512 devices in a mesh: ev: 8 (over y, core), mem: 64 (over x, z).
Axes of the slice: x: 4, y: 4, z: 16, core: 2. Of those that a mesh axis runs over, the one named last changes fastest.
Arguments:
- memory: bfloat16 [131072, 512], P(('ev', 'mem')), may hold values from -24 to 24
- last_time: int32 [131072], P(('ev', 'mem')), may hold values from 0 to 499
- event_time: int32 [65536], P(('ev', 'mem')), may hold values from 500 to 999
- edge_features: bfloat16 [65536, 48], P(('ev', 'mem')), may hold values from -6 to 6
- update_slot: int32 [65536, 2], P(('ev', 'mem')), may hold values from 0 to 1023, as said below
- update_serve: int32 [512, 1024], P(('ev', 'mem')), may hold values from -1 to 255, as said below
- lookup_slot: int32 [65536, 7], P(('ev', 'mem')), may hold values from 0 to 1535, as said below
- lookup_serve: int32 [512, 1536], P(('ev', 'mem')), may hold values from -1 to 255, as said below
- neighbour_gap: int32 [65536, 10], P(('ev', 'mem')), may hold values from 0 to 999
- hub_node: int32 [512], P(('ev', 'mem')), may hold values from 0 to 255
- hub_choice: int32 [65536, 4], P(('ev', 'mem')), may hold values from 0 to 511
- time_freq: float32 [100], replicated, may hold values from 0.001 to 0.3
- time_phase: float32 [100], replicated, may hold values from -3.140625 to 3.140625
- gru_weight: bfloat16 [1684, 1536], P(None, 'ev'), may hold values from -0.1875 to 0.1875
- gru_bias: float32 [2, 1536], replicated, may hold values from -3 to 3
- query_weight: bfloat16 [612, 256], replicated, may hold values from -0.25 to 0.25
- keyval_weight: bfloat16 [612, 512], replicated, may hold values from -0.25 to 0.25
- output_weight: bfloat16 [768, 512], replicated, may hold values from -0.21875 to 0.21875
Outputs:
- new_memory: bfloat16 [131072, 512], P(('ev', 'mem'))
- embedding: bfloat16 [65536, 512], P(('ev', 'mem'))
The draws below stay inside these ranges and needn't reach their ends.
Inputs may be any that keep to these rules, and one draw needn't show every extreme that they name: Within one device's events the values of update_slot are distinct; at most 2 of one device's endpoints go to one owner, and one owner, drawn from the seed, gets exactly 2 from every device. update_serve holds a local node exactly in the slots named by update_slot, -1 elsewhere; several slots may name the same node. Within one device's queries the values of lookup_slot are distinct; at most 3 of one device's lookups go to one owner, and one owner gets exactly 3 from every device. lookup_serve holds a local node exactly in the slots named by lookup_slot, -1 elsewhere.
All inputs are finite; a program needn't handle non-finite values.
Results may differ from the reference program's by a relative error of at most 0.011.
Values may be sent and summed in bfloat16 or wider, within the bound.
A program may use at most 64 MiB of HBM per device.

```python
import math
import jax
import jax.numpy as jnp
from jax import lax

MEMW = 512
TW = 100
EF = 48
MSG = 1172
KEYW = 612
ATT = 256
HEADS = 2
HSIZE = 128
KN = 10
KHUB = 4
KROUTE = 7
EV_DEV = 128
NODE_DEV = 256
HUB_DEV = 1
HUBS = 512
EVENTS = 65536
NODES = 131072
CAP = 2
CAPN = 3
DEVICES = 512


def route_tables(key, capacity, columns):
    slot_total = DEVICES * capacity
    hot_owner = jax.random.randint(jax.random.fold_in(key, 7), (), 0, DEVICES)
    owners = jnp.arange(slot_total, dtype=jnp.int32) // capacity

    def for_device(device):
        dev_key = jax.random.fold_in(key, device + 100)
        ranking = jax.random.permutation(jax.random.fold_in(dev_key, 1), slot_total).astype(jnp.int32)
        ranking = jnp.where(owners == hot_owner, jnp.arange(slot_total, dtype=jnp.int32) % capacity - capacity, ranking)
        order = jnp.argsort(ranking, stable=True).astype(jnp.int32)
        chosen = order[:EV_DEV * columns]
        shuffle = jax.random.permutation(jax.random.fold_in(dev_key, 2), EV_DEV * columns)
        targets = chosen[shuffle]
        node_local = jax.random.randint(jax.random.fold_in(dev_key, 3), (slot_total,), 0, NODE_DEV)
        marked = jnp.zeros((slot_total,), jnp.int32).at[chosen].set(1)
        serving = jnp.where(marked > 0, node_local, -1).astype(jnp.int32)
        return (targets, serving)
    targets, serving = jax.vmap(for_device)(jnp.arange(DEVICES, dtype=jnp.int32))
    targets = targets.reshape(DEVICES * EV_DEV, columns).astype(jnp.int32)
    serving = serving.reshape(DEVICES, DEVICES, capacity).transpose(1, 0, 2).reshape(DEVICES, DEVICES * capacity)
    return (targets, serving)


def draw_update_slot(key, part):
    return route_tables(jax.random.fold_in(key, 11), CAP, 2)[0]


def draw_update_serve(key, part):
    return route_tables(jax.random.fold_in(key, 11), CAP, 2)[1]


def draw_lookup_slot(key, part):
    return route_tables(jax.random.fold_in(key, 13), CAPN, KROUTE)[0]


def draw_lookup_serve(key, part):
    return route_tables(jax.random.fold_in(key, 13), CAPN, KROUTE)[1]


def draw_memory(key, part):
    values = jnp.clip(jax.random.normal(jax.random.fold_in(key, 23), (NODES, MEMW), jnp.float32), -4.0, 4.0)
    return values.astype(jnp.bfloat16)


def touch_ends(array, own_key, smallest, top_value):
    longest = array.shape.index(max(array.shape))
    spots = []
    for shift in (0, 1):
        where = [jax.random.randint(jax.random.fold_in(own_key, axis), (), 0, length) for axis, length in enumerate(array.shape)]
        where[longest] = (where[longest] + shift) % array.shape[longest]
        spots.append(tuple(where))
    return array.at[spots[0]].set(smallest).at[spots[1]].set(top_value)


def shard_levels(rng, shape, pieces, least, top_value):
    gain = 1.0
    for dim, parts in pieces:
        steps = jax.random.uniform(jax.random.fold_in(jax.random.fold_in(rng, 6), dim), (parts,), jnp.float32, least / len(pieces), top_value / len(pieces))
        gain = gain * jnp.repeat(jnp.exp(steps), shape[dim] // parts).reshape((-1,) + (1,) * (len(shape) - 1 - dim))
    return gain


def scatter_about(stream_key, dims, spread, limit, pieces=(), kind=jnp.bfloat16):
    factor_of = shard_levels(stream_key, dims, pieces, -0.22, 0.18) if pieces else 1.0
    entries = jax.random.normal(stream_key, dims, jnp.float32) * spread * factor_of
    return jnp.minimum(jnp.maximum(entries, -limit), limit).astype(kind)


def setup_inputs(seed: int = 0) -> dict:
    key_of = jax.random.split(jax.random.key(seed), 19)
    memory = draw_memory(jax.random.fold_in(key_of[18], 71), 0)
    last_time = touch_ends(jax.random.randint(key_of[1], (NODES,), 0, 500), jax.random.fold_in(key_of[1], 1), 0, 499).astype(jnp.int32)
    event_time = touch_ends(jax.random.randint(key_of[2], (EVENTS,), 500, 1000), jax.random.fold_in(key_of[2], 1), 500, 999).astype(jnp.int32)
    edge_features = scatter_about(key_of[3], (EVENTS, EF), 1.0, 6.0, ((0, 512),))
    update_slot = draw_update_slot(jax.random.fold_in(key_of[18], 71), 0)
    update_serve = draw_update_serve(jax.random.fold_in(key_of[18], 71), 0)
    lookup_slot = draw_lookup_slot(jax.random.fold_in(key_of[18], 71), 0)
    lookup_serve = draw_lookup_serve(jax.random.fold_in(key_of[18], 71), 0)
    neighbour_gap = touch_ends(jax.random.randint(key_of[8], (EVENTS, KN), 0, 1000), jax.random.fold_in(key_of[8], 1), 0, 999).astype(jnp.int32)
    hub_node = touch_ends(jax.random.randint(key_of[9], (HUBS,), 0, NODE_DEV), jax.random.fold_in(key_of[9], 1), 0, NODE_DEV - 1).astype(jnp.int32)
    hub_choice = touch_ends(jax.random.randint(key_of[10], (EVENTS, KHUB), 0, HUBS), jax.random.fold_in(key_of[10], 1), 0, HUBS - 1).astype(jnp.int32)
    time_freq = jnp.clip(jnp.exp(jax.random.uniform(key_of[11], (TW,), jnp.float32, math.log(0.001), math.log(0.3))), 0.001, 0.3)
    time_phase = jnp.clip(jax.random.uniform(key_of[12], (TW,), jnp.float32, -3.140625, 3.140625), -3.140625, 3.140625)
    gru_weight = scatter_about(key_of[13], (MSG + MEMW, 3 * MEMW), MSG ** -0.5, 0.1875, ((1, 8),))
    gru_bias = scatter_about(key_of[14], (2, 3 * MEMW), 0.5, 3.0, (), jnp.float32)
    query_weight = scatter_about(key_of[15], (KEYW, ATT), KEYW ** -0.5, 0.25)
    keyval_weight = scatter_about(key_of[16], (KEYW, 2 * ATT), KEYW ** -0.5, 0.25)
    output_weight = scatter_about(key_of[17], (ATT + MEMW, MEMW), (ATT + MEMW) ** -0.5, 0.21875)
    return {"memory": memory, "last_time": last_time, "event_time": event_time, "edge_features": edge_features, "update_slot": update_slot, "update_serve": update_serve, "lookup_slot": lookup_slot, "lookup_serve": lookup_serve, "neighbour_gap": neighbour_gap, "hub_node": hub_node, "hub_choice": hub_choice, "time_freq": time_freq, "time_phase": time_phase, "gru_weight": gru_weight, "gru_bias": gru_bias, "query_weight": query_weight, "keyval_weight": keyval_weight, "output_weight": output_weight}


def encode(gap, time_freq, time_phase):
    return jnp.cos(gap.astype(jnp.float32)[..., None] * time_freq + time_phase).astype(jnp.bfloat16)


def gru_update(pre_in, pre_hid, previous_mem, counts):
    mem_width = previous_mem.shape[1]
    reset_gate = jax.nn.sigmoid(pre_in[:, :mem_width] + pre_hid[:, :mem_width])
    update_gate = jax.nn.sigmoid(pre_in[:, mem_width:2 * mem_width] + pre_hid[:, mem_width:2 * mem_width])
    candidate = jnp.tanh(pre_in[:, 2 * mem_width:] + reset_gate * pre_hid[:, 2 * mem_width:])
    previous = previous_mem.astype(jnp.float32)
    fresh = (1.0 - update_gate) * candidate + update_gate * previous
    return jnp.where(counts[:, None] > 0, fresh, previous).astype(jnp.bfloat16)


def node_ids(slot_table, serve_table, capacity):
    rows = slot_table.shape[0]
    device = (jnp.arange(rows, dtype=jnp.int32) // EV_DEV)[:, None]
    owner = slot_table // capacity
    slot = slot_table % capacity
    local = serve_table[owner, device * capacity + slot]
    return (owner * NODE_DEV + local).astype(jnp.int32)


def reference(memory, last_time, event_time, edge_features, update_slot, update_serve, lookup_slot, lookup_serve, neighbour_gap, hub_node, hub_choice, time_freq, time_phase, gru_weight, gru_bias, query_weight, keyval_weight, output_weight):
    ids_update = node_ids(update_slot, update_serve, CAP)
    device_rows = jnp.broadcast_to((jnp.arange(EVENTS, dtype=jnp.int32) // EV_DEV)[:, None], (EVENTS, 2))
    inverse = jnp.full((DEVICES, DEVICES * CAP), -1, jnp.int32)
    inverse = inverse.at[device_rows, update_slot].set(jnp.arange(EVENTS * 2, dtype=jnp.int32).reshape(EVENTS, 2))

    def owner_block(owner):
        column = jnp.arange(DEVICES * CAP, dtype=jnp.int32)
        requester = column // CAP
        slot = column % CAP
        endpoint = jnp.maximum(inverse[requester, owner * CAP + slot], 0)
        event = endpoint // 2
        side = endpoint % 2
        own_node = ids_update[event, side]
        other_node = ids_update[event, 1 - side]
        encoded = encode(event_time[event] - last_time[own_node], time_freq, time_phase)
        message = jnp.concatenate([memory[own_node], memory[other_node], encoded, edge_features[event]], axis=1)
        local = update_serve[owner]
        matches = jnp.arange(NODE_DEV, dtype=jnp.int32)[:, None] == local[None, :]
        summed = jnp.dot(matches.astype(jnp.bfloat16), message, preferred_element_type=jnp.float32)
        counts = jnp.sum(matches.astype(jnp.float32), axis=1)
        averaged = (summed / jnp.maximum(counts, 1.0)[:, None]).astype(jnp.bfloat16)
        block_mem = lax.dynamic_slice_in_dim(memory, owner * NODE_DEV, NODE_DEV, 0)
        pre_in = jnp.dot(averaged, gru_weight[:MSG], preferred_element_type=jnp.float32) + gru_bias[0]
        pre_hid = jnp.dot(block_mem, gru_weight[MSG:], preferred_element_type=jnp.float32) + gru_bias[1]
        return gru_update(pre_in, pre_hid, block_mem, counts)

    new_memory = lax.map(owner_block, jnp.arange(DEVICES, dtype=jnp.int32)).reshape(NODES, MEMW)
    hub_ids = ((jnp.arange(HUBS, dtype=jnp.int32) // HUB_DEV) * NODE_DEV + hub_node).astype(jnp.int32)
    hub_table = new_memory[hub_ids]
    ids_lookup = node_ids(lookup_slot, lookup_serve, CAPN)

    def event_block(device):
        start = (device * EV_DEV).astype(jnp.int32)
        block_ids = lax.dynamic_slice_in_dim(ids_lookup, start, EV_DEV, 0)
        block_hubs = lax.dynamic_slice_in_dim(hub_choice, start, EV_DEV, 0)
        block_gap = lax.dynamic_slice_in_dim(neighbour_gap, start, EV_DEV, 0)
        looked = new_memory[block_ids]
        self_row = looked[:, 0]
        neighbours = jnp.concatenate([looked[:, 1:], hub_table[block_hubs]], axis=1)
        key_input = jnp.concatenate([neighbours, encode(block_gap, time_freq, time_phase)], axis=2).reshape(EV_DEV * KN, KEYW)
        keyval = jnp.dot(key_input, keyval_weight, preferred_element_type=jnp.float32).astype(jnp.bfloat16).reshape(EV_DEV, KN, 2 * ATT)
        self_enc = encode(jnp.zeros((EV_DEV,), jnp.int32), time_freq, time_phase)
        queries = jnp.dot(jnp.concatenate([self_row, self_enc], axis=1), query_weight, preferred_element_type=jnp.float32).astype(jnp.bfloat16)
        query_heads = queries.reshape(EV_DEV, HEADS, HSIZE).astype(jnp.float32)
        key_heads = keyval[:, :, :ATT].reshape(EV_DEV, KN, HEADS, HSIZE).astype(jnp.float32)
        value_heads = keyval[:, :, ATT:].reshape(EV_DEV, KN, HEADS, HSIZE).astype(jnp.float32)
        scores = jnp.einsum("ehd,ekhd->ehk", query_heads, key_heads) * (HSIZE ** -0.5)
        scores = scores - jnp.max(scores, axis=2, keepdims=True)
        expo = jnp.exp(scores)
        prob = (expo / jnp.sum(expo, axis=2, keepdims=True)).astype(jnp.bfloat16)
        mixed = jnp.einsum("ehk,ekhd->ehd", prob.astype(jnp.float32), value_heads).astype(jnp.bfloat16).reshape(EV_DEV, ATT)
        return jnp.dot(jnp.concatenate([mixed, self_row], axis=1), output_weight, preferred_element_type=jnp.float32).astype(jnp.bfloat16)

    embedding = lax.map(event_block, jnp.arange(DEVICES, dtype=jnp.int32)).reshape(EVENTS, MEMW)
    return new_memory, embedding
```

```python
import jax
import jax.numpy as jnp
from jax import lax
from jax.sharding import PartitionSpec as P

HEADS = 2
DIGIT = 32
BF = jnp.bfloat16
F32 = jnp.float32


def encode(gap, time_freq, time_phase):
    return jnp.cos(gap.astype(F32)[..., None] * time_freq + time_phase).astype(BF)


def dot(a, b):
    return jnp.dot(a, b, preferred_element_type=F32)


def one_hot(index, size):
    return (index[:, None] == jnp.arange(size, dtype=jnp.int32)[None, :]).astype(BF)


def exchange(rows, ev_size, mem_size):
    total, width = rows.shape
    cap = total // (ev_size * mem_size)
    near = lax.all_to_all(
        rows.reshape(ev_size, mem_size * cap, width), "ev", split_axis=0, concat_axis=0, tiled=True
    )
    near = near.reshape(ev_size, mem_size, cap, width).transpose(1, 0, 2, 3)
    far = lax.all_to_all(
        near.reshape(mem_size, ev_size * cap, width), "mem", split_axis=0, concat_axis=0, tiled=True
    )
    return far.reshape(total, width)


def arrival(slot, cap, ev_size, mem_size):
    device, at = slot // cap, slot % cap
    return (device % mem_size) * (ev_size * cap) + (device // mem_size) * cap + at


def local(
    memory,
    last_time,
    event_time,
    edge_features,
    update_slot,
    update_serve,
    lookup_slot,
    lookup_serve,
    neighbour_gap,
    hub_node,
    hub_choice,
    time_freq,
    time_phase,
    gru_weight,
    gru_bias,
    query_weight,
    keyval_weight,
    output_weight,
):
    ev_size = lax.axis_size("ev")
    mem_size = lax.axis_size("mem")
    devices = ev_size * mem_size
    node_count, width = memory.shape
    event_count = event_time.shape[0]
    edge_width = edge_features.shape[1]
    time_width = time_freq.shape[0]

    weight = lax.all_gather(gru_weight, "ev", axis=1, tiled=True)

    serve = update_serve[0]
    total = serve.shape[0]
    cap = total // devices
    fetched = exchange(dot(one_hot(serve, node_count), memory).astype(BF), ev_size, mem_size)

    other_slot = update_slot[:, ::-1].reshape(-1)
    other = dot(one_hot(arrival(other_slot, cap, ev_size, mem_size), total), fetched).astype(BF)
    digits = jnp.stack([event_time // DIGIT, event_time % DIGIT], axis=1).astype(BF)
    extra = jnp.concatenate([edge_features, digits], axis=1)
    extra = jnp.pad(extra, ((0, 0), (0, 128 - extra.shape[1])))
    extra = jnp.broadcast_to(extra[:, None], (event_count, 2, 128)).reshape(2 * event_count, 128)
    slots = update_slot.reshape(-1)
    place = (jnp.arange(total, dtype=jnp.int32)[:, None] == slots[None, :]).astype(BF)
    outgoing = dot(place, jnp.concatenate([other, extra], axis=1)).astype(BF)
    received = exchange(outgoing, ev_size, mem_size)

    serve_in = serve.reshape(ev_size, mem_size, cap).transpose(1, 0, 2).reshape(-1)
    matches = jnp.arange(node_count, dtype=jnp.int32)[:, None] == serve_in[None, :]
    counts = jnp.sum(matches.astype(F32), axis=1)
    before = jnp.sum(jnp.where(matches, last_time.astype(F32)[:, None], 0.0), axis=0)
    tail = received[:, width:].astype(F32)
    when = tail[:, edge_width] * DIGIT + tail[:, edge_width + 1]
    encoded = encode(when - before, time_freq, time_phase)
    arrived = jnp.concatenate(
        [received[:, :width], encoded, received[:, width : width + edge_width]], axis=1
    )
    summed = dot(matches.astype(BF), arrived)
    averaged = (summed / jnp.maximum(counts, 1.0)[:, None]).astype(BF)
    rest = width + averaged.shape[1]
    pre_in = dot(memory, weight[:width]) + dot(averaged, weight[width:rest]) + gru_bias[0]
    pre_hid = dot(memory, weight[rest:]) + gru_bias[1]
    reset = jax.nn.sigmoid(pre_in[:, :width] + pre_hid[:, :width])
    update = jax.nn.sigmoid(pre_in[:, width : 2 * width] + pre_hid[:, width : 2 * width])
    candidate = jnp.tanh(pre_in[:, 2 * width :] + reset * pre_hid[:, 2 * width :])
    previous = memory.astype(F32)
    fresh = (1.0 - update) * candidate + update * previous
    new_memory = jnp.where(counts[:, None] > 0, fresh, previous).astype(BF)

    hub = dot(one_hot(hub_node, node_count), new_memory).astype(BF)
    hub_table = lax.all_gather(hub, "mem", axis=0, tiled=True)
    hub_table = lax.all_gather(hub_table, "ev", axis=0, tiled=True)

    serve = lookup_serve[0]
    total = serve.shape[0]
    cap = total // devices
    looked = exchange(dot(one_hot(serve, node_count), new_memory).astype(BF), ev_size, mem_size)

    places = arrival(lookup_slot.T.reshape(-1), cap, ev_size, mem_size)
    routed = dot(one_hot(places, total), looked).astype(BF)
    picked = dot(one_hot(hub_choice.T.reshape(-1), hub_table.shape[0]), hub_table).astype(BF)
    self_row = routed[:event_count]
    neighbours = jnp.concatenate([routed[event_count:], picked], axis=0)
    gaps = encode(neighbour_gap.T.reshape(-1), time_freq, time_phase)
    keyval = (dot(neighbours, keyval_weight[:width]) + dot(gaps, keyval_weight[width:])).astype(BF)
    keyval = keyval.reshape(-1, event_count, keyval.shape[1])
    self_enc = encode(jnp.zeros((1,), jnp.int32), time_freq, time_phase)
    query = (dot(self_row, query_weight[:width]) + dot(self_enc, query_weight[width:])).astype(BF)
    att_width = query_weight.shape[1]
    head = att_width // HEADS
    mixed = []
    for h in range(HEADS):
        q = query[:, h * head : (h + 1) * head].astype(F32)
        k = keyval[:, :, h * head : (h + 1) * head].astype(F32)
        v = keyval[:, :, att_width + h * head : att_width + (h + 1) * head].astype(F32)
        scores = jnp.sum(q[None] * k, axis=2) * head ** (-0.5)
        scores = scores - jnp.max(scores, axis=0, keepdims=True)
        expo = jnp.exp(scores)
        prob = (expo / jnp.sum(expo, axis=0, keepdims=True)).astype(BF)
        mixed.append(jnp.sum(prob.astype(F32)[:, :, None] * v, axis=0).astype(BF))
    mixed = jnp.concatenate(mixed, axis=1)
    embedding = (dot(mixed, output_weight[:att_width]) + dot(self_row, output_weight[att_width:])).astype(BF)
    return (new_memory, embedding)


def solution(mesh):
    both = ("ev", "mem")
    rows, flat = P(both, None), P(both)
    return jax.shard_map(
        local,
        mesh=mesh,
        in_specs=(
            rows, flat, flat, rows, rows, rows, rows, rows, rows, flat, rows,
            P(), P(), P(None, "ev"), P(), P(), P(), P(),
        ),
        out_specs=(rows, rows),
        check_vma=False,
    )
```

```python
import functools

import jax
import jax.numpy as jnp
from jax import lax
from jax.experimental import pallas as pl
from jax.experimental.pallas import tpu as pltpu
from jax.sharding import PartitionSpec as P

HEADS = 2
DIGIT = 32
EV, MEM, ZS, XS = 8, 64, 16, 4
DEVICES = EV * MEM
CAP, CAPN = 2, 3
MESH = pl.DeviceIdType.MESH
BF = jnp.bfloat16
F32 = jnp.float32
I32 = jnp.int32


def encode(gap, time_freq, time_phase):
    return jnp.cos(gap.astype(F32)[..., None] * time_freq + time_phase).astype(BF)


def dot(a, b):
    return jnp.dot(a, b, preferred_element_type=F32)


def one_hot(index, size):
    return (index[:, None] == jnp.arange(size, dtype=I32)[None, :]).astype(BF)


def mask_bf(mask):
    return jnp.where(mask, 1.0, 0.0).astype(BF)


def iota(shape, dim):
    return lax.broadcasted_iota(I32, shape, dim)


def div(x, k):
    if k % 3 == 0:
        return ((x // (k // 3)) * 43691) >> 17
    return x // k


def place():
    e, m = lax.axis_index("ev"), lax.axis_index("mem")
    return e, m, m // ZS, lax.rem(m, ZS)


def greet():
    e, m, _, _ = place()
    barrier = pltpu.get_barrier_semaphore()

    def near(i, carry):
        pl.semaphore_signal(barrier, inc=1, device_id=(lax.rem(e + i, EV), m), device_id_type=MESH)
        return carry

    def far(i, carry):
        pl.semaphore_signal(barrier, inc=1, device_id=(e, lax.rem(m + i, MEM)), device_id_type=MESH)
        return carry

    lax.fori_loop(1, EV, near, 0)
    lax.fori_loop(1, MEM, far, 0)
    pl.semaphore_wait(barrier, EV + MEM - 2)


def landed(ref, sem):
    pltpu.make_async_copy(ref, ref, sem).wait()


def send_near(chunk, source, near, sent, came):
    e, m, _, _ = place()
    pltpu.make_async_copy(source.at[chunk, e], near.at[chunk, e], came.at[chunk]).start()

    def step(i, carry):
        t = lax.rem(e + i, EV)
        pltpu.make_async_remote_copy(
            source.at[chunk, t], near.at[chunk, e], sent, came.at[chunk],
            device_id=(t, m), device_id_type=MESH,
        ).start()
        return carry

    lax.fori_loop(1, EV, step, 0)


def reorder(slots):
    n = EV * ZS * slots
    row, col = iota((n, n), 0), iota((n, n), 1)
    z, rest = div(row, EV * slots), row
    rest = row - z * (EV * slots)
    e = div(rest, slots)
    s = rest - e * slots
    return mask_bf(col == e * (ZS * slots) + z * slots + s)


def send_far(chunk, slots, perm, near, staged, result, sent, came):
    e, m, _, mz = place()
    rows = EV * ZS * slots
    width = near.shape[-1]
    landed(near.at[chunk], came[0].at[chunk])
    block = dot(perm, near[chunk].reshape(rows, width)).astype(BF)
    staged[pl.ds(chunk * ZS, ZS)] = block.reshape(ZS, EV * slots, width)

    def step(i, carry):
        t = chunk * ZS + lax.rem(mz + i, ZS)

        @pl.when(t != m)
        def _():
            pltpu.make_async_remote_copy(
                staged.at[t], result.at[m], sent, came[1], device_id=(e, t), device_id_type=MESH
            ).start()

        return carry

    lax.fori_loop(0, ZS, step, 0)


def finish_own(staged, result, came):
    _, m, _, _ = place()
    pltpu.make_async_copy(staged.at[m], result.at[m], came).start()


def drain(source, result, sent_near, sent_far):
    for c in range(XS):
        landed(source.at[c, pl.ds(0, EV - 1)], sent_near)
    landed(result.at[pl.ds(0, MEM - 1)], sent_far)


def update_kernel(
    memory, serve, other_at, slots, extra, weight_own,
    received, tails, weights,
    xf, nf, sf, rf, xm, nm, sm, xe, ne, se,
    f1s, f1r, f2s, f2r, m1s, m1r, m2s, m2r, e1s, e1r, e2s, e2r, ws, wr, cs, cr,
):
    e, m, mx, _ = place()
    nodes = memory.shape[0]
    width = memory.shape[1]
    rows = EV * ZS * CAP
    for c in range(XS):
        pick = serve[pl.ds(c * rows, rows), :] == iota((rows, nodes), 1)
        xf[c] = dot(mask_bf(pick), memory[...]).astype(BF).reshape(EV, ZS * CAP, width)
        target = iota((rows // CAP, 1), 0)
        target = ((target // ZS) * MEM + c * ZS + lax.rem(target, ZS)) * CAP
        first = dot(mask_bf(target == slots[...]), extra[...])
        second = dot(mask_bf(target + 1 == slots[...]), extra[...])
        half = extra.shape[1] // 2
        tail = jnp.where(iota(first.shape, 1) < half, first, second)
        xe[c] = tail.astype(BF).reshape(EV, ZS, extra.shape[1])
    perm = reorder(CAP)
    perm_one = reorder(1)
    greet()
    for c in range(XS):
        send_near(lax.rem(mx + c, XS), xf, nf, f1s, f1r)
    for c in range(XS):
        send_near(lax.rem(mx + c, XS), xe, ne, e1s, e1r)
    own = pltpu.make_async_copy(weight_own, weights.at[e], cs)
    own.start()
    for hop in range(1, EV // 2):
        pltpu.make_async_remote_copy(
            weight_own, weights.at[e], ws, wr,
            device_id=(lax.rem(e + 2 * hop, EV), m), device_id_type=MESH,
        ).start()
    for c in range(XS):
        chunk = lax.rem(mx + c, XS)
        send_far(chunk, CAP, perm, nf, sf, rf, f2s, (f1r, f2r))
        send_far(chunk, 1, perm_one, ne, se, tails, e2s, (e1r, e2r))
    finish_own(sf, rf, f2r)
    finish_own(se, tails, e2r)
    landed(weights.at[pl.ds(0, EV // 2 - 1)], wr)
    own.wait()
    partner = e + 1 - 2 * lax.rem(e, 2)
    for hop in range(EV // 2):
        block = lax.rem(e + 2 * hop, EV)
        pltpu.make_async_remote_copy(
            weights.at[block], weights.at[block], ws, cr,
            device_id=(partner, m), device_id_type=MESH,
        ).start()
    landed(rf, f2r)
    total = MEM * EV * CAP
    pick = mask_bf(other_at[...] == iota((other_at.shape[0], total), 1))
    other = dot(pick, rf[...].reshape(total, width)).astype(BF)
    for c in range(XS):
        chunk = lax.rem(mx + c, XS)
        target = iota((rows, 1), 0)
        target = (target // (ZS * CAP)) * (MEM * CAP) + chunk * (ZS * CAP) + lax.rem(target, ZS * CAP)
        block = dot(mask_bf(target == slots[...]), other).astype(BF)
        xm[chunk] = block.reshape(EV, ZS * CAP, width)
        send_near(chunk, xm, nm, m1s, m1r)
    for c in range(XS):
        send_far(lax.rem(mx + c, XS), CAP, perm, nm, sm, received, m2s, (m1r, m2r))
    finish_own(sm, received, m2r)
    landed(tails, e2r)
    landed(weights.at[pl.ds(0, EV // 2)], cr)
    landed(received, m2r)
    drain(xf, rf, f1s, f2s)
    drain(xe, tails, e1s, e2s)
    drain(xm, received, m1s, m2s)
    landed(weights.at[pl.ds(0, EV - 1)], ws)


def lookup_kernel(
    new_memory, serve, hub, looked, hubs,
    xl, nl, sl, hub_all, l1s, l1r, l2s, l2r, h1s, h1r, h2s, h2r,
):
    e, m, mx, _ = place()
    nodes, width = new_memory.shape
    rows = EV * ZS * CAPN
    for c in range(XS):
        pick = serve[pl.ds(c * rows, rows), :] == iota((rows, nodes), 1)
        xl[c] = dot(mask_bf(pick), new_memory[...]).astype(BF).reshape(EV, ZS * CAPN, width)
    perm = reorder(CAPN)
    greet()
    for c in range(XS):
        send_near(lax.rem(mx + c, XS), xl, nl, l1s, l1r)
    pltpu.make_async_copy(hub, hub_all.at[m], h1r).start()

    def step(i, carry):
        t = lax.rem(m + i, MEM)
        pltpu.make_async_remote_copy(
            hub, hub_all.at[m], h1s, h1r, device_id=(e, t), device_id_type=MESH
        ).start()
        return carry

    lax.fori_loop(1, MEM, step, 0)
    for c in range(XS):
        send_far(lax.rem(mx + c, XS), CAPN, perm, nl, sl, looked, l2s, (l1r, l2r))
    finish_own(sl, looked, l2r)
    landed(hub_all, h1r)
    pltpu.make_async_copy(hub_all, hubs.at[e], h2r).start()

    def near(i, carry):
        t = lax.rem(e + i, EV)
        pltpu.make_async_remote_copy(
            hub_all, hubs.at[e], h2s, h2r, device_id=(t, m), device_id_type=MESH
        ).start()
        return carry

    lax.fori_loop(1, EV, near, 0)
    landed(hubs, h2r)
    landed(looked, l2r)
    drain(xl, looked, l1s, l2s)
    landed(hub_all.at[pl.ds(0, MEM - 1)], h1s)
    landed(hubs.at[pl.ds(0, EV - 1)], h2s)


def vm(*shape):
    return pltpu.VMEM(shape, BF)


def path(slots, width):
    return [
        vm(XS, EV, ZS * slots, width),
        vm(XS, EV, ZS * slots, width),
        vm(MEM, EV * slots, width),
    ]


def sems():
    dma = pltpu.SemaphoreType.DMA
    return [dma, dma((XS,)), dma, dma]


def run(kernel, shapes, scratch, ident, *args):
    spec = pl.BlockSpec(memory_space=pltpu.VMEM)
    return pl.pallas_call(
        kernel,
        out_shape=[jax.ShapeDtypeStruct(s, BF) for s in shapes],
        in_specs=[spec] * len(args),
        out_specs=[spec] * len(shapes),
        scratch_shapes=scratch,
        compiler_params=pltpu.CompilerParams(
            collective_id=ident, has_side_effects=True, vmem_limit_bytes=60 << 20
        ),
    )(*args)


def chunked(table, slots):
    return table.reshape(EV, XS, ZS * slots).transpose(1, 0, 2).reshape(-1, 1)


def arrival(slot, cap):
    device, at = slot // cap, slot % cap
    return (device % MEM) * (EV * cap) + (device // MEM) * cap + at


def local(
    memory,
    last_time,
    event_time,
    edge_features,
    update_slot,
    update_serve,
    lookup_slot,
    lookup_serve,
    neighbour_gap,
    hub_node,
    hub_choice,
    time_freq,
    time_phase,
    gru_weight,
    gru_bias,
    query_weight,
    keyval_weight,
    output_weight,
):
    node_count, width = memory.shape
    event_count = event_time.shape[0]
    edge_width = edge_features.shape[1]
    time_width = time_freq.shape[0]
    msg_width = 2 * width + time_width + edge_width
    gates = gru_weight.shape[1] * EV

    serve = update_serve[0]
    other_at = arrival(update_slot[:, ::-1].reshape(-1, 1), CAP)
    digits = jnp.stack([event_time // DIGIT, event_time % DIGIT], axis=1).astype(BF)
    extra = jnp.concatenate([edge_features, digits], axis=1)
    extra = jnp.pad(extra, ((0, 0), (0, 64 - extra.shape[1])))
    extra = jnp.broadcast_to(extra[:, None, None], (event_count, 2, 2, 64)).reshape(2 * event_count, 128)
    weight_t = gru_weight.T
    weight_t = jnp.concatenate(
        [weight_t[:, : 2 * width], weight_t[:, msg_width:], weight_t[:, 2 * width : msg_width],
         jnp.zeros((weight_t.shape[0], 256 - time_width - edge_width), BF)], axis=1
    )
    received, tails, weights = run(
        update_kernel,
        [(MEM, EV * CAP, width), (MEM, EV, 128), (EV,) + weight_t.shape],
        path(CAP, width) + [vm(MEM, EV * CAP, width)] + path(CAP, width) + path(1, 128)
        + sems() + sems() + sems() + [pltpu.SemaphoreType.DMA] * 4,
        0,
        memory, chunked(serve, CAP), other_at, update_slot.reshape(1, -1), extra, weight_t,
    )
    weight = weights.reshape(gates, -1)

    def through(rows, first, size):
        return lax.dot_general(
            rows, weight[:, first : first + size], (((1,), (1,)), ((), ())), preferred_element_type=F32
        )

    serve_in = serve.reshape(EV, MEM, CAP).transpose(1, 0, 2)
    nodes = jnp.arange(node_count, dtype=I32)[:, None]
    matches = nodes == serve_in.reshape(1, -1)
    counts = jnp.sum(matches.astype(F32), axis=1)
    summed = dot(matches.astype(BF), received.reshape(-1, width))
    tails = tails.reshape(-1, 128)
    tail_sum = 0.0
    for s in range(CAP):
        part = tails[:, s * 64 : s * 64 + 64]
        hits = nodes == serve_in[:, :, s].reshape(1, -1)
        before = jnp.sum(jnp.where(hits, last_time.astype(F32)[:, None], 0.0), axis=0)
        when = part[:, edge_width].astype(F32) * DIGIT + part[:, edge_width + 1].astype(F32)
        both = jnp.concatenate([encode(when - before, time_freq, time_phase), part[:, :edge_width]], axis=1)
        tail_sum = tail_sum + dot(hits.astype(BF), both)
    share = jnp.maximum(counts, 1.0)[:, None]
    averaged = (summed / share).astype(BF)
    tail_mean = (tail_sum / share).astype(BF)
    pre_in = (
        through(memory, 0, width) + through(averaged, width, width)
        + through(tail_mean, 3 * width, time_width + edge_width) + gru_bias[0]
    )
    pre_hid = through(memory, 2 * width, width) + gru_bias[1]
    reset = jax.nn.sigmoid(pre_in[:, :width] + pre_hid[:, :width])
    update = jax.nn.sigmoid(pre_in[:, width : 2 * width] + pre_hid[:, width : 2 * width])
    candidate = jnp.tanh(pre_in[:, 2 * width :] + reset * pre_hid[:, 2 * width :])
    previous = memory.astype(F32)
    fresh = (1.0 - update) * candidate + update * previous
    new_memory = jnp.where(counts[:, None] > 0, fresh, previous).astype(BF)

    hub = dot(one_hot(hub_node, node_count), new_memory).astype(BF).reshape(4, 128)
    dma = pltpu.SemaphoreType.DMA
    looked, hubs = run(
        lookup_kernel,
        [(MEM, EV * CAPN, width), (EV, MEM, 4, 128)],
        path(CAPN, width) + [vm(MEM, 4, 128)] + sems() + [dma] * 4,
        1,
        new_memory, chunked(lookup_serve[0], CAPN), hub,
    )
    looked = looked.reshape(-1, width)
    hub_table = hubs.reshape(-1, width)

    places = arrival(lookup_slot.T.reshape(-1), CAPN)
    routed = dot(one_hot(places, looked.shape[0]), looked).astype(BF)
    picked = dot(one_hot(hub_choice.T.reshape(-1), hub_table.shape[0]), hub_table).astype(BF)
    self_row = routed[:event_count]
    neighbours = jnp.concatenate([routed[event_count:], picked], axis=0)
    gaps = encode(neighbour_gap.T.reshape(-1), time_freq, time_phase)
    keyval = (dot(neighbours, keyval_weight[:width]) + dot(gaps, keyval_weight[width:])).astype(BF)
    keyval = keyval.reshape(-1, event_count, keyval.shape[1])
    self_enc = encode(jnp.zeros((1,), I32), time_freq, time_phase)
    query = (dot(self_row, query_weight[:width]) + dot(self_enc, query_weight[width:])).astype(BF)
    att_width = query_weight.shape[1]
    head = att_width // HEADS
    mixed = []
    for h in range(HEADS):
        q = query[:, h * head : (h + 1) * head].astype(F32)
        k = keyval[:, :, h * head : (h + 1) * head].astype(F32)
        v = keyval[:, :, att_width + h * head : att_width + (h + 1) * head].astype(F32)
        scores = jnp.sum(q[None] * k, axis=2) * head ** (-0.5)
        scores = scores - jnp.max(scores, axis=0, keepdims=True)
        expo = jnp.exp(scores)
        prob = (expo / jnp.sum(expo, axis=0, keepdims=True)).astype(BF)
        mixed.append(jnp.sum(prob.astype(F32)[:, :, None] * v, axis=0).astype(BF))
    mixed = jnp.concatenate(mixed, axis=1)
    embedding = (dot(mixed, output_weight[:att_width]) + dot(self_row, output_weight[att_width:])).astype(BF)
    return (new_memory, embedding)


def solution(mesh):
    both = ("ev", "mem")
    rows, flat = P(both, None), P(both)
    return jax.shard_map(
        local,
        mesh=mesh,
        in_specs=(
            rows, flat, flat, rows, rows, rows, rows, rows, rows, flat, rows,
            P(), P(), P(None, "ev"), P(), P(), P(), P(),
        ),
        out_specs=(rows, rows),
        check_vma=False,
    )
```

```python
import functools

import jax
import jax.numpy as jnp
from jax import lax
from jax.experimental import pallas as pl
from jax.experimental.pallas import tpu as pltpu
from jax.sharding import PartitionSpec as P

HEADS = 2
DIGIT = 32
EV, MEM, ZS, XS = 8, 64, 16, 4
DEVICES = EV * MEM
CAP, CAPN = 2, 3
MESH = pl.DeviceIdType.MESH
BF = jnp.bfloat16
F32 = jnp.float32
I32 = jnp.int32


def dot(a, b):
    return jnp.dot(a, b, preferred_element_type=F32)


def dot_t(a, b):
    return lax.dot_general(a, b, (((1,), (1,)), ((), ())), preferred_element_type=F32)


def mask_bf(mask):
    return jnp.where(mask, 1.0, 0.0).astype(BF)


def iota(shape, dim):
    return lax.broadcasted_iota(I32, shape, dim)


def div(x, k):
    if k % 3 == 0:
        return ((x // (k // 3)) * 43691) >> 17
    return x // k


def place():
    e, m = lax.axis_index("ev"), lax.axis_index("mem")
    return e, m, m // ZS, lax.rem(m, ZS)


def greet():
    e, m, _, _ = place()
    barrier = pltpu.get_barrier_semaphore()

    def near(i, carry):
        pl.semaphore_signal(barrier, inc=1, device_id=(lax.rem(e + i, EV), m), device_id_type=MESH)
        return carry

    def far(i, carry):
        pl.semaphore_signal(barrier, inc=1, device_id=(e, lax.rem(m + i, MEM)), device_id_type=MESH)
        return carry

    lax.fori_loop(1, EV, near, 0)
    lax.fori_loop(1, MEM, far, 0)


def meet():
    pl.semaphore_wait(pltpu.get_barrier_semaphore(), EV + MEM - 2)


def landed(ref, sem):
    pltpu.make_async_copy(ref, ref, sem).wait()


def send_near(chunk, source, near, sent, came):
    e, m, _, _ = place()
    pltpu.make_async_copy(source.at[chunk, e], near.at[chunk, e], came.at[chunk]).start()

    def step(i, carry):
        t = lax.rem(e + i, EV)
        pltpu.make_async_remote_copy(
            source.at[chunk, t], near.at[chunk, e], sent, came.at[chunk],
            device_id=(t, m), device_id_type=MESH,
        ).start()
        return carry

    lax.fori_loop(1, EV, step, 0)


def reorder(slots):
    n = EV * ZS * slots
    row, col = iota((n, n), 0), iota((n, n), 1)
    z, rest = div(row, EV * slots), row
    rest = row - z * (EV * slots)
    e = div(rest, slots)
    s = rest - e * slots
    return mask_bf(col == e * (ZS * slots) + z * slots + s)


def send_far(chunk, slots, perm, near, staged, result, sent, came):
    e, m, _, mz = place()
    rows = EV * ZS * slots
    width = near.shape[-1]
    landed(near.at[chunk], came[0].at[chunk])
    block = dot(perm, near[chunk].reshape(rows, width)).astype(BF)
    staged[pl.ds(chunk * ZS, ZS)] = block.reshape(ZS, EV * slots, width)

    def step(i, carry):
        t = chunk * ZS + lax.rem(mz + i, ZS)

        @pl.when(t != m)
        def _():
            pltpu.make_async_remote_copy(
                staged.at[t], result.at[m], sent, came[1], device_id=(e, t), device_id_type=MESH
            ).start()

        return carry

    lax.fori_loop(0, ZS, step, 0)


def finish_own(staged, result, came):
    _, m, _, _ = place()
    pltpu.make_async_copy(staged.at[m], result.at[m], came).start()


def drain(source, result, sent_near, sent_far):
    for c in range(XS):
        landed(source.at[c, pl.ds(0, EV - 1)], sent_near)
    landed(result.at[pl.ds(0, MEM - 1)], sent_far)


def column(row):
    eye = iota((128, 128), 0) == iota((128, 128), 1)
    parts = []
    for b in range(row.shape[1] // 128):
        piece = row[:, b * 128 : b * 128 + 128].astype(F32)
        parts.append(jnp.sum(jnp.where(eye, piece, 0.0), axis=1, keepdims=True))
    return jnp.concatenate(parts, axis=0).astype(I32)


def arrival(slot, cap):
    device = div(slot, cap)
    at = slot - device * cap
    return (device % MEM) * (EV * cap) + (device // MEM) * cap + at


def spread(rows, slots):
    return rows.reshape(EV, XS, ZS * slots, rows.shape[1])


def encode(gap, freq, phase):
    return jnp.cos(gap.astype(F32) * freq + phase).astype(BF)


def step_kernel(
    memory, last_time, event_time, edge, update_slot, update_serve, lookup_slot, lookup_serve,
    neighbour_gap, hub_node, hub_choice, freq, phase, weight, bias, query_weight, keyval_weight,
    output_weight,
    new_memory, embedding,
    xf, nf, sf, rf, xm, nm, sm, rm, xe, ne, se, tails, xl, nl, sl, looked,
    shard, weights, gather, matches, pre_in, pre_hid, hub_one, hub_all, hub_rows, hubs, keyenc, keyhub,
    query_enc, gather_look,
    f1s, f1r, f2s, f2r, e1s, e1r, e2s, e2r, m1s, m1r, m2s, m2r, l1s, l1r, l2s, l2r,
    ws, wr, cs, cr, h1s, h1r, h2s, h2r,
):
    e, m, mx, _ = place()
    nodes, width = memory.shape
    events = event_time.shape[1]
    edges = edge.shape[0]
    times = freq.shape[1]
    total = MEM * EV * CAP
    total_look = MEM * EV * CAPN
    order = [lax.rem(mx + c, XS) for c in range(XS)]

    greet()
    pick = column(update_serve[...]) == iota((total, nodes), 1)
    rows = spread(dot(mask_bf(pick), memory[...]).astype(BF), CAP)
    for c in range(XS):
        xf[c] = rows[:, c]
    meet()
    for chunk in order:
        send_near(chunk, xf, nf, f1s, f1r)

    when = event_time[...]
    late = when // DIGIT
    packed = jnp.concatenate(
        [edge[...].astype(F32), late.astype(F32), (when - late * DIGIT).astype(F32),
         jnp.zeros((64 - edges - 2, events), F32)], axis=0
    )
    extra = jnp.concatenate([packed, packed], axis=0).T.astype(BF)
    slots = update_slot[...]
    target = iota((total // CAP, events), 0) * CAP
    tail = [
        dot(mask_bf((target + s == slots[0:1]) | (target + s == slots[1:2])), extra) for s in range(CAP)
    ]
    tail = jnp.where(iota(tail[0].shape, 1) < 64, tail[0], tail[1]).astype(BF)
    tail = spread(tail, 1)
    for c in range(XS):
        xe[c] = tail[:, c]
    for chunk in order:
        send_near(chunk, xe, ne, e1s, e1r)

    shard[:, 0 : 2 * width] = weight[:, 0 : 2 * width]
    rest = weight.shape[1] - 2 * width
    row, col = iota((rest, width + 256), 0), iota((rest, width + 256), 1)
    source = jnp.where(
        col < width, col + times + edges,
        jnp.where(col < width + 128, jnp.where(col < width + times, col - width, -1),
                  jnp.where(col < width + 128 + edges, col - width - 128 + times, -1)))
    shard[:, 2 * width :] = dot(weight[:, 2 * width :], mask_bf(row == source)).astype(BF)
    block = shard.shape[0]

    def part(index):
        return weights.at[pl.ds(pl.multiple_of(index * block, block), block)]

    own = pltpu.make_async_copy(shard, part(e), cs)
    own.start()
    for hop in range(1, EV // 2):
        pltpu.make_async_remote_copy(
            shard, part(e), ws, wr,
            device_id=(lax.rem(e + 2 * hop, EV), m), device_id_type=MESH,
        ).start()

    perm = reorder(CAP)
    perm_one = reorder(1)
    for chunk in order:
        send_far(chunk, CAP, perm, nf, sf, rf, f2s, (f1r, f2r))
        send_far(chunk, 1, perm_one, ne, se, tails, e2s, (e1r, e2r))
    finish_own(sf, rf, f2r)
    finish_own(se, tails, e2r)

    places = arrival(slots, CAP)
    places = column(jnp.concatenate([places[1:2], places[0:1]], axis=1))
    gather[...] = mask_bf(places == iota((2 * events, total), 1))
    serve = jnp.broadcast_to(update_serve[...].astype(F32), (16, total)).astype(BF)
    row, col = iota((total, total), 0), iota((total, total), 1)
    col = ((col // CAP) % EV) * (MEM * CAP) + (col // (CAP * EV)) * CAP + col % CAP
    serve_in = dot(serve, mask_bf(row == col))[0:1].astype(I32)
    met = serve_in == iota((nodes, total), 0)
    matches[...] = mask_bf(met)
    counts = jnp.sum(jnp.where(met, 1.0, 0.0), axis=1, keepdims=True)
    share = jnp.maximum(counts, 1.0)
    row, col = iota((total, total // CAP), 0), iota((total, total // CAP), 1)
    col = (col % EV) * (MEM * CAP) + (col // EV) * CAP
    serve_of = [dot(serve, mask_bf(row == col + s))[0:1].astype(I32) for s in range(CAP)]

    landed(weights.at[pl.ds(0, (EV // 2 - 1) * block)], wr)
    own.wait()
    partner = e + 1 - 2 * lax.rem(e, 2)
    for hop in range(EV // 2):
        index = lax.rem(e + 2 * hop, EV)
        pltpu.make_async_remote_copy(
            part(index), part(index), ws, cr, device_id=(partner, m), device_id_type=MESH
        ).start()

    landed(rf, f2r)
    other = dot(gather[...], rf[...].reshape(total, width)).astype(BF)
    slot_row = jnp.concatenate([slots[0:1], slots[1:2]], axis=1)
    for chunk in order:
        target = iota((EV * ZS * CAP, 1), 0)
        target = (target // (ZS * CAP)) * (MEM * CAP) + chunk * (ZS * CAP) + target % (ZS * CAP)
        message = dot(mask_bf(target == slot_row), other).astype(BF)
        xm[chunk] = message.reshape(EV, ZS * CAP, width)
        send_near(chunk, xm, nm, m1s, m1r)
    for chunk in order:
        send_far(chunk, CAP, perm, nm, sm, rm, m2s, (m1r, m2r))
    finish_own(sm, rm, m2r)

    landed(weights.at[pl.ds(0, EV // 2 * block)], cr)
    landed(tails, e2r)
    arrived = tails[...].reshape(total // CAP, 128)
    encoded_sum, edge_sum = 0.0, []
    for s in range(CAP):
        hits = serve_of[s] == iota((nodes, total // CAP), 0)
        mine = column(serve_of[s]) == iota((total // CAP, nodes), 1)
        before = jnp.sum(jnp.where(mine, last_time[...].astype(F32), 0.0), axis=1, keepdims=True)
        digits = arrived[:, s * 64 : s * 64 + 64].astype(F32)
        time = digits[:, edges : edges + 1] * DIGIT + digits[:, edges + 1 : edges + 2]
        encoded = jnp.cos((time - before) * freq[...] + phase[...]).astype(BF)
        encoded_sum = encoded_sum + dot(mask_bf(hits), encoded)
        edge_sum.append(dot(mask_bf(hits), arrived))
    edge_sum = edge_sum[0] + pltpu.roll(edge_sum[1], 64, 1)
    encoded_mean = (encoded_sum / share).astype(BF)
    edge_mean = (edge_sum / share).astype(BF)
    w = 3 * width
    for t in range(3):
        third = pl.ds(t * width, width)
        pre_in[:, third] = (
            dot_t(memory[...], weights[third, 0:width])
            + dot_t(encoded_mean, weights[third, w : w + times])
            + dot_t(edge_mean, weights[third, w + 128 : w + 256])
            + bias[0:1, third]
        )
        pre_hid[:, third] = dot_t(memory[...], weights[third, 2 * width : 3 * width]) + bias[1:2, third]

    landed(rm, m2r)
    summed = dot(matches[...], rm[...].reshape(total, width))
    averaged = (summed / share).astype(BF)

    def pre(t):
        third = pl.ds(t * width, width)
        return pre_in[:, third] + dot_t(averaged, weights[third, width : 2 * width])

    reset = jax.nn.sigmoid(pre(0) + pre_hid[:, 0:width])
    update = jax.nn.sigmoid(pre(1) + pre_hid[:, width : 2 * width])
    candidate = jnp.tanh(pre(2) + reset * pre_hid[:, 2 * width : 3 * width])
    previous = memory[...].astype(F32)
    fresh = (1.0 - update) * candidate + update * previous
    new_memory[...] = jnp.where(counts > 0, fresh, previous).astype(BF)

    pick = column(lookup_serve[...]) == iota((total_look, nodes), 1)
    rows = spread(dot(mask_bf(pick), new_memory[...]).astype(BF), CAPN)
    for c in range(XS):
        xl[c] = rows[:, c]
    for chunk in order:
        send_near(chunk, xl, nl, l1s, l1r)
    hub = dot(mask_bf(hub_node[...] == iota((16, nodes), 1)), new_memory[...])
    hub_one[...] = jnp.concatenate(
        [hub[0:1, j * 128 : j * 128 + 128] for j in range(width // 128)], axis=0
    ).astype(BF)
    pltpu.make_async_copy(hub_one, hub_all.at[m], h1r).start()

    def hub_far(i, carry):
        t = lax.rem(m + i, MEM)
        pltpu.make_async_remote_copy(
            hub_one, hub_all.at[m], h1s, h1r, device_id=(e, t), device_id_type=MESH
        ).start()
        return carry

    lax.fori_loop(1, MEM, hub_far, 0)
    perm = reorder(CAPN)
    for chunk in order:
        send_far(chunk, CAPN, perm, nl, sl, looked, l2s, (l1r, l2r))
    finish_own(sl, looked, l2r)
    landed(hub_all, h1r)
    gathered = hub_all[...].astype(F32)
    hub_rows[...] = jnp.concatenate(
        [gathered[:, j, :] for j in range(width // 128)], axis=1
    ).astype(BF)
    pltpu.make_async_copy(hub_rows, hubs.at[e], h2r).start()

    def hub_near(i, carry):
        pltpu.make_async_remote_copy(
            hub_rows, hubs.at[e], h2s, h2r, device_id=(lax.rem(e + i, EV), m), device_id_type=MESH
        ).start()
        return carry

    lax.fori_loop(1, EV, hub_near, 0)

    routed = lookup_slot.shape[0]
    near = neighbour_gap.shape[0]
    for k in range(near):
        encoded = encode(column(neighbour_gap[k : k + 1]), freq[...], phase[...])
        keyenc[k] = dot(encoded, keyval_weight[width : width + times])
    still = jnp.broadcast_to(jnp.cos(phase[...]), (16, times)).astype(BF)
    query_enc[...] = dot(still, query_weight[width : width + times])
    for k in range(routed):
        at = column(arrival(lookup_slot[k : k + 1], CAPN))
        gather_look[pl.ds(k * events, events)] = mask_bf(at == iota((events, total_look), 1))
    landed(hubs, h2r)
    for k in range(near - routed + 1):
        choice = column(hub_choice[k : k + 1])
        rows = dot(mask_bf(choice == iota((events, DEVICES), 1)), hubs[...].reshape(DEVICES, width)).astype(BF)
        keyhub[k] = (dot(rows, keyval_weight[0:width]) + keyenc[routed - 1 + k]).astype(BF)

    landed(looked, l2r)
    everything = looked[...].reshape(total_look, width)
    own_row = dot(gather_look[0:events], everything).astype(BF)
    query = (dot(own_row, query_weight[0:width]) + query_enc[0:1]).astype(BF).astype(F32)
    att = query.shape[1]
    head = att // HEADS
    keyval = []
    for k in range(near):
        if k < routed - 1:
            rows = dot(gather_look[pl.ds((k + 1) * events, events)], everything).astype(BF)
            keyval.append((dot(rows, keyval_weight[0:width]) + keyenc[k]).astype(BF))
        else:
            keyval.append(keyhub[k - routed + 1])
    mixed = []
    for h in range(HEADS):
        q = query[:, h * head : h * head + head]
        scores = [
            jnp.sum(q * kv[:, h * head : h * head + head].astype(F32), axis=1, keepdims=True)
            * head ** (-0.5)
            for kv in keyval
        ]
        top = functools.reduce(jnp.maximum, scores)
        expo = [jnp.exp(x - top) for x in scores]
        base = functools.reduce(jnp.add, expo)
        acc = 0.0
        for x, kv in zip(expo, keyval):
            prob = (x / base).astype(BF).astype(F32)
            acc = acc + prob * kv[:, att + h * head : att + h * head + head].astype(F32)
        mixed.append(acc.astype(BF))
    mixed = jnp.concatenate(mixed, axis=1)
    embedding[...] = (
        dot(mixed, output_weight[0:att]) + dot(own_row, output_weight[att : att + width])
    ).astype(BF)

    drain(xf, rf, f1s, f2s)
    drain(xe, tails, e1s, e2s)
    drain(xm, rm, m1s, m2s)
    drain(xl, looked, l1s, l2s)
    landed(weights.at[pl.ds(0, (EV - 1) * block)], ws)
    landed(hub_all.at[pl.ds(0, MEM - 1)], h1s)
    landed(hubs.at[pl.ds(0, EV - 1)], h2s)


def vm(*shape, dtype=BF):
    return pltpu.VMEM(shape, dtype)


def path(slots, width):
    near = (XS, EV, ZS * slots, width)
    far = (MEM, EV * slots, width)
    return [vm(*near), vm(*near), vm(*far), vm(*far)]


def sems():
    dma = pltpu.SemaphoreType.DMA
    return [dma, dma((XS,)), dma, dma]


def local(
    memory,
    last_time,
    event_time,
    edge_features,
    update_slot,
    update_serve,
    lookup_slot,
    lookup_serve,
    neighbour_gap,
    hub_node,
    hub_choice,
    time_freq,
    time_phase,
    gru_weight,
    gru_bias,
    query_weight,
    keyval_weight,
    output_weight,
):
    nodes, width = memory.shape
    events = event_time.shape[0]
    gates = gru_bias.shape[1]
    padded = 3 * width + 256
    routed = lookup_slot.shape[1]
    near = neighbour_gap.shape[1]
    total, total_look = update_serve.shape[1], lookup_serve.shape[1]
    args = (
        memory, last_time.reshape(1, -1), event_time.reshape(1, -1), edge_features.T, update_slot.T,
        update_serve, lookup_slot.T, lookup_serve, neighbour_gap.T, hub_node.reshape(1, 1),
        hub_choice.T, time_freq.reshape(1, -1), time_phase.reshape(1, -1), gru_weight.T, gru_bias,
        query_weight, keyval_weight, output_weight,
    )
    spec = pl.BlockSpec(memory_space=pltpu.VMEM)
    dma = pltpu.SemaphoreType.DMA
    return tuple(pl.pallas_call(
        step_kernel,
        out_shape=[
            jax.ShapeDtypeStruct((nodes, width), BF),
            jax.ShapeDtypeStruct((events, width), BF),
        ],
        in_specs=[spec] * len(args),
        out_specs=[spec] * 2,
        scratch_shapes=path(CAP, width) + path(CAP, width) + path(1, 128) + path(CAPN, width)
        + [
            vm(gates // EV, padded),
            vm(gates, padded),
            vm(2 * events, total),
            vm(nodes, total),
            vm(nodes, gates, dtype=F32),
            vm(nodes, gates, dtype=F32),
            vm(width // 128, 128),
            vm(MEM, width // 128, 128),
            vm(MEM, width),
            vm(EV, MEM, width),
            vm(near, events, keyval_weight.shape[1], dtype=F32),
            vm(near - routed + 1, events, keyval_weight.shape[1]),
            vm(16, query_weight.shape[1], dtype=F32),
            vm(routed * events, total_look),
        ]
        + sems() * 4 + [dma] * 8,
        compiler_params=pltpu.CompilerParams(
            collective_id=0, has_side_effects=True, vmem_limit_bytes=62 << 20
        ),
    )(*args))


def solution(mesh):
    both = ("ev", "mem")
    rows, flat = P(both, None), P(both)
    return jax.shard_map(
        local,
        mesh=mesh,
        in_specs=(
            rows, flat, flat, rows, rows, rows, rows, rows, rows, flat, rows,
            P(), P(), P(None, "ev"), P(), P(), P(), P(),
        ),
        out_specs=(rows, rows),
        check_vma=False,
    )
```

```python
import functools

import jax
import jax.numpy as jnp
from jax import lax
from jax.experimental import pallas as pl
from jax.experimental.pallas import tpu as pltpu
from jax.sharding import PartitionSpec as P

HEADS = 2
DIGIT = 32
EV, MEM, ZS, XS = 8, 64, 16, 4
DEVICES = EV * MEM
CAP, CAPN = 2, 3
MESH = pl.DeviceIdType.MESH
BF = jnp.bfloat16
F32 = jnp.float32
I32 = jnp.int32


def dot(a, b):
    return jnp.dot(a, b, preferred_element_type=F32)


def dot_t(a, b):
    return lax.dot_general(a, b, (((1,), (1,)), ((), ())), preferred_element_type=F32)


def mask_bf(mask):
    return jnp.where(mask, 1.0, 0.0).astype(BF)


def iota(shape, dim):
    return lax.broadcasted_iota(I32, shape, dim)


def div(x, k):
    if k % 3 == 0:
        return ((x // (k // 3)) * 43691) >> 17
    return x // k


def place():
    e, m = lax.axis_index("ev"), lax.axis_index("mem")
    return e, m, m // ZS, lax.rem(m, ZS)


def greet():
    e, m, _, _ = place()
    barrier = pltpu.get_barrier_semaphore()

    def near(i, carry):
        pl.semaphore_signal(barrier, inc=1, device_id=(lax.rem(e + i, EV), m), device_id_type=MESH)
        return carry

    def far(i, carry):
        pl.semaphore_signal(barrier, inc=1, device_id=(e, lax.rem(m + i, MEM)), device_id_type=MESH)
        return carry

    lax.fori_loop(1, EV, near, 0)
    lax.fori_loop(1, MEM, far, 0)


def meet():
    pl.semaphore_wait(pltpu.get_barrier_semaphore(), EV + MEM - 2)


def landed(ref, sem):
    pltpu.make_async_copy(ref, ref, sem).wait()


def send_near(chunk, source, near, sent, came):
    e, m, _, _ = place()
    pltpu.make_async_copy(source.at[chunk, e], near.at[chunk, e], came.at[chunk]).start()

    def step(i, carry):
        t = lax.rem(e + i, EV)
        pltpu.make_async_remote_copy(
            source.at[chunk, t], near.at[chunk, e], sent, came.at[chunk],
            device_id=(t, m), device_id_type=MESH,
        ).start()
        return carry

    lax.fori_loop(1, EV, step, 0)


def reorder(slots):
    n = EV * ZS * slots
    row, col = iota((n, n), 0), iota((n, n), 1)
    z, rest = div(row, EV * slots), row
    rest = row - z * (EV * slots)
    e = div(rest, slots)
    s = rest - e * slots
    return mask_bf(col == e * (ZS * slots) + z * slots + s)


def send_far(chunk, slots, perm, near, staged, result, sent, came):
    e, m, _, mz = place()
    rows = EV * ZS * slots
    width = near.shape[-1]
    landed(near.at[chunk], came[0].at[chunk])
    block = dot(perm, near[chunk].reshape(rows, width)).astype(BF)
    staged[pl.ds(chunk * ZS, ZS)] = block.reshape(ZS, EV * slots, width)

    def step(i, carry):
        t = chunk * ZS + lax.rem(mz + i, ZS)

        @pl.when(t != m)
        def _():
            pltpu.make_async_remote_copy(
                staged.at[t], result.at[m], sent, came[1], device_id=(e, t), device_id_type=MESH
            ).start()

        return carry

    lax.fori_loop(0, ZS, step, 0)


def finish_own(staged, result, came):
    _, m, _, _ = place()
    pltpu.make_async_copy(staged.at[m], result.at[m], came).start()


def drain(source, result, sent_near, sent_far):
    for c in range(XS):
        landed(source.at[c, pl.ds(0, EV - 1)], sent_near)
    landed(result.at[pl.ds(0, MEM - 1)], sent_far)


def column(row):
    eye = iota((128, 128), 0) == iota((128, 128), 1)
    parts = []
    for b in range(row.shape[1] // 128):
        piece = row[:, b * 128 : b * 128 + 128].astype(F32)
        parts.append(jnp.sum(jnp.where(eye, piece, 0.0), axis=1, keepdims=True))
    return jnp.concatenate(parts, axis=0).astype(I32)


def arrival(slot, cap):
    device = div(slot, cap)
    at = slot - device * cap
    return (device % MEM) * (EV * cap) + (device // MEM) * cap + at


def spread(rows, slots):
    return rows.reshape(EV, XS, ZS * slots, rows.shape[1])


def encode(gap, freq, phase):
    return jnp.cos(gap.astype(F32) * freq + phase).astype(BF)


def step_kernel(
    memory_in, last_time, event_time, edge, update_slot, update_serve, lookup_slot, lookup_serve,
    neighbour_gap, hub_node, hub_choice, freq, phase, weight_in, bias, query_weight_in, keyval_weight_in,
    output_weight_in,
    new_memory_out, embedding,
    xf, nf, sf, rf, xm, nm, sm, rm, xe, ne, se, tails, xl, nl, sl, looked,
    shard, weights, gather, matches, pre_in, pre_hid, hub_one, hub_all, hub_rows, hubs, keyenc, keyhub,
    query_enc, gather_look, serve_look, route, memory, weight, query_weight, keyval_weight,
    output_weight, new_memory,
    f1s, f1r, f2s, f2r, e1s, e1r, e2s, e2r, m1s, m1r, m2s, m2r, l1s, l1r, l2s, l2r,
    ws, wr, cs, cr, h1s, h1r, h2s, h2r, load, store,
):
    e, m, mx, _ = place()
    nodes, width = memory.shape
    events = event_time.shape[1]
    edges = edge.shape[0]
    times = freq.shape[1]
    total = MEM * EV * CAP
    total_look = MEM * EV * CAPN
    order = [lax.rem(mx + c, XS) for c in range(XS)]

    greet()
    loads = [
        pltpu.make_async_copy(a, b, load.at[i])
        for i, (a, b) in enumerate([
            (memory_in, memory), (weight_in, weight), (query_weight_in, query_weight),
            (keyval_weight_in, keyval_weight), (output_weight_in, output_weight),
        ])
    ]
    for copy in loads:
        copy.start()
    pick = column(update_serve[...]) == iota((total, nodes), 1)
    loads[0].wait()
    rows = spread(dot(mask_bf(pick), memory[...]).astype(BF), CAP)
    for c in range(XS):
        xf[c] = rows[:, c]
    meet()
    for chunk in order:
        send_near(chunk, xf, nf, f1s, f1r)

    when = event_time[...]
    late = when // DIGIT
    packed = jnp.concatenate(
        [edge[...].astype(F32), late.astype(F32), (when - late * DIGIT).astype(F32),
         jnp.zeros((64 - edges - 2, events), F32)], axis=0
    )
    extra = jnp.concatenate([packed, packed], axis=0).T.astype(BF)
    slots = update_slot[...]
    target = iota((total // CAP, events), 0) * CAP
    tail = [
        dot(mask_bf((target + s == slots[0:1]) | (target + s == slots[1:2])), extra) for s in range(CAP)
    ]
    tail = jnp.where(iota(tail[0].shape, 1) < 64, tail[0], tail[1]).astype(BF)
    tail = spread(tail, 1)
    for c in range(XS):
        xe[c] = tail[:, c]
    for chunk in order:
        send_near(chunk, xe, ne, e1s, e1r)

    loads[1].wait()
    shard[:, 0 : 2 * width] = weight[:, 0 : 2 * width]
    rest = weight.shape[1] - 2 * width
    row, col = iota((rest, width + 256), 0), iota((rest, width + 256), 1)
    source = jnp.where(
        col < width, col + times + edges,
        jnp.where(col < width + 128, jnp.where(col < width + times, col - width, -1),
                  jnp.where(col < width + 128 + edges, col - width - 128 + times, -1)))
    shard[:, 2 * width :] = dot(weight[:, 2 * width :], mask_bf(row == source)).astype(BF)
    block = shard.shape[0]

    def part(index):
        return weights.at[pl.ds(pl.multiple_of(index * block, block), block)]

    own = pltpu.make_async_copy(shard, part(e), cs)
    own.start()
    for hop in range(1, EV // 2):
        pltpu.make_async_remote_copy(
            shard, part(e), ws, wr,
            device_id=(lax.rem(e + 2 * hop, EV), m), device_id_type=MESH,
        ).start()

    perm = reorder(CAP)
    perm_one = reorder(1)
    for chunk in order:
        send_far(chunk, CAP, perm, nf, sf, rf, f2s, (f1r, f2r))
    for chunk in order:
        send_far(chunk, 1, perm_one, ne, se, tails, e2s, (e1r, e2r))
    finish_own(sf, rf, f2r)
    finish_own(se, tails, e2r)

    places = arrival(slots, CAP)
    places = column(jnp.concatenate([places[1:2], places[0:1]], axis=1))
    gather[...] = mask_bf(places == iota((2 * events, total), 1))
    slot_row = jnp.concatenate([slots[0:1], slots[1:2]], axis=1)
    for c in range(XS):
        target = iota((EV * ZS * CAP, 1), 0)
        target = (target // (ZS * CAP)) * (MEM * CAP) + c * (ZS * CAP) + target % (ZS * CAP)
        route[c] = dot(mask_bf(target == slot_row), gather[...]).astype(BF)
    serve = jnp.broadcast_to(update_serve[...].astype(F32), (16, total)).astype(BF)
    row, col = iota((total, total), 0), iota((total, total), 1)
    col = ((col // CAP) % EV) * (MEM * CAP) + (col // (CAP * EV)) * CAP + col % CAP
    serve_in = dot(serve, mask_bf(row == col))[0:1].astype(I32)
    met = serve_in == iota((nodes, total), 0)
    matches[...] = mask_bf(met)
    counts = jnp.sum(jnp.where(met, 1.0, 0.0), axis=1, keepdims=True)
    share = jnp.maximum(counts, 1.0)
    row, col = iota((total, total // CAP), 0), iota((total, total // CAP), 1)
    col = (col % EV) * (MEM * CAP) + (col // EV) * CAP
    serve_of = [dot(serve, mask_bf(row == col + s))[0:1].astype(I32) for s in range(CAP)]

    landed(weights.at[pl.ds(0, (EV // 2 - 1) * block)], wr)
    own.wait()
    partner = e + 1 - 2 * lax.rem(e, 2)
    for hop in range(EV // 2):
        index = lax.rem(e + 2 * hop, EV)
        pltpu.make_async_remote_copy(
            part(index), part(index), ws, cr, device_id=(partner, m), device_id_type=MESH
        ).start()

    landed(rf, f2r)
    for chunk in order:
        message = dot(route[chunk], rf[...].reshape(total, width)).astype(BF)
        xm[chunk] = message.reshape(EV, ZS * CAP, width)
        send_near(chunk, xm, nm, m1s, m1r)
    for chunk in order:
        send_far(chunk, CAP, perm, nm, sm, rm, m2s, (m1r, m2r))
    finish_own(sm, rm, m2r)

    landed(weights.at[pl.ds(0, EV // 2 * block)], cr)
    landed(tails, e2r)
    arrived = tails[...].reshape(total // CAP, 128)
    encoded_sum, edge_sum = 0.0, []
    for s in range(CAP):
        hits = serve_of[s] == iota((nodes, total // CAP), 0)
        mine = column(serve_of[s]) == iota((total // CAP, nodes), 1)
        before = jnp.sum(jnp.where(mine, last_time[...].astype(F32), 0.0), axis=1, keepdims=True)
        digits = arrived[:, s * 64 : s * 64 + 64].astype(F32)
        time = digits[:, edges : edges + 1] * DIGIT + digits[:, edges + 1 : edges + 2]
        encoded = jnp.cos((time - before) * freq[...] + phase[...]).astype(BF)
        encoded_sum = encoded_sum + dot(mask_bf(hits), encoded)
        edge_sum.append(dot(mask_bf(hits), arrived))
    edge_sum = edge_sum[0] + pltpu.roll(edge_sum[1], 64, 1)
    encoded_mean = (encoded_sum / share).astype(BF)
    edge_mean = (edge_sum / share).astype(BF)
    w = 3 * width
    for t in range(3):
        third = pl.ds(t * width, width)
        pre_in[:, third] = (
            dot_t(memory[...], weights[third, 0:width])
            + dot_t(encoded_mean, weights[third, w : w + times])
            + dot_t(edge_mean, weights[third, w + 128 : w + 256])
            + bias[0:1, third]
        )
        pre_hid[:, third] = dot_t(memory[...], weights[third, 2 * width : 3 * width]) + bias[1:2, third]
    serve_look[...] = mask_bf(column(lookup_serve[...]) == iota((total_look, nodes), 1))
    perm = reorder(CAPN)

    landed(rm, m2r)
    summed = dot(matches[...], rm[...].reshape(total, width))
    averaged = (summed / share).astype(BF)

    def pre(t):
        third = pl.ds(t * width, width)
        return pre_in[:, third] + dot_t(averaged, weights[third, width : 2 * width])

    reset = jax.nn.sigmoid(pre(0) + pre_hid[:, 0:width])
    update = jax.nn.sigmoid(pre(1) + pre_hid[:, width : 2 * width])
    candidate = jnp.tanh(pre(2) + reset * pre_hid[:, 2 * width : 3 * width])
    previous = memory[...].astype(F32)
    fresh = (1.0 - update) * candidate + update * previous
    new_memory[...] = jnp.where(counts > 0, fresh, previous).astype(BF)

    rows = spread(dot(serve_look[...], new_memory[...]).astype(BF), CAPN)
    for c in range(XS):
        xl[c] = rows[:, c]
    for chunk in order:
        send_near(chunk, xl, nl, l1s, l1r)
    result = pltpu.make_async_copy(new_memory, new_memory_out, store)
    result.start()
    hub = dot(mask_bf(hub_node[...] == iota((16, nodes), 1)), new_memory[...])
    hub_one[...] = jnp.concatenate(
        [hub[0:1, j * 128 : j * 128 + 128] for j in range(width // 128)], axis=0
    ).astype(BF)
    pltpu.make_async_copy(hub_one, hub_all.at[m], h1r).start()

    def hub_far(i, carry):
        t = lax.rem(m + i, MEM)
        pltpu.make_async_remote_copy(
            hub_one, hub_all.at[m], h1s, h1r, device_id=(e, t), device_id_type=MESH
        ).start()
        return carry

    lax.fori_loop(1, MEM, hub_far, 0)
    for chunk in order:
        send_far(chunk, CAPN, perm, nl, sl, looked, l2s, (l1r, l2r))
    finish_own(sl, looked, l2r)
    landed(hub_all, h1r)
    gathered = hub_all[...].astype(F32)
    hub_rows[...] = jnp.concatenate(
        [gathered[:, j, :] for j in range(width // 128)], axis=1
    ).astype(BF)
    pltpu.make_async_copy(hub_rows, hubs.at[e], h2r).start()

    def hub_near(i, carry):
        pltpu.make_async_remote_copy(
            hub_rows, hubs.at[e], h2s, h2r, device_id=(lax.rem(e + i, EV), m), device_id_type=MESH
        ).start()
        return carry

    lax.fori_loop(1, EV, hub_near, 0)

    routed = lookup_slot.shape[0]
    near = neighbour_gap.shape[0]
    for copy in loads[2:]:
        copy.wait()
    for k in range(near):
        encoded = encode(column(neighbour_gap[k : k + 1]), freq[...], phase[...])
        keyenc[k] = dot(encoded, keyval_weight[width : width + times])
    still = jnp.broadcast_to(jnp.cos(phase[...]), (16, times)).astype(BF)
    query_enc[...] = dot(still, query_weight[width : width + times])
    for k in range(routed):
        at = column(arrival(lookup_slot[k : k + 1], CAPN))
        gather_look[pl.ds(k * events, events)] = mask_bf(at == iota((events, total_look), 1))
    landed(hubs, h2r)
    for k in range(near - routed + 1):
        choice = column(hub_choice[k : k + 1])
        rows = dot(mask_bf(choice == iota((events, DEVICES), 1)), hubs[...].reshape(DEVICES, width)).astype(BF)
        keyhub[k] = (dot(rows, keyval_weight[0:width]) + keyenc[routed - 1 + k]).astype(BF)

    landed(looked, l2r)
    everything = looked[...].reshape(total_look, width)
    own_row = dot(gather_look[0:events], everything).astype(BF)
    query = (dot(own_row, query_weight[0:width]) + query_enc[0:1]).astype(BF).astype(F32)
    att = query.shape[1]
    head = att // HEADS
    keyval = []
    for k in range(near):
        if k < routed - 1:
            rows = dot(gather_look[pl.ds((k + 1) * events, events)], everything).astype(BF)
            keyval.append((dot(rows, keyval_weight[0:width]) + keyenc[k]).astype(BF))
        else:
            keyval.append(keyhub[k - routed + 1])
    mixed = []
    for h in range(HEADS):
        q = query[:, h * head : h * head + head]
        scores = [
            jnp.sum(q * kv[:, h * head : h * head + head].astype(F32), axis=1, keepdims=True)
            * head ** (-0.5)
            for kv in keyval
        ]
        top = functools.reduce(jnp.maximum, scores)
        expo = [jnp.exp(x - top) for x in scores]
        base = functools.reduce(jnp.add, expo)
        acc = 0.0
        for x, kv in zip(expo, keyval):
            prob = (x / base).astype(BF).astype(F32)
            acc = acc + prob * kv[:, att + h * head : att + h * head + head].astype(F32)
        mixed.append(acc.astype(BF))
    mixed = jnp.concatenate(mixed, axis=1)
    embedding[...] = (
        dot(mixed, output_weight[0:att]) + dot(own_row, output_weight[att : att + width])
    ).astype(BF)

    drain(xf, rf, f1s, f2s)
    drain(xe, tails, e1s, e2s)
    drain(xm, rm, m1s, m2s)
    drain(xl, looked, l1s, l2s)
    landed(weights.at[pl.ds(0, (EV - 1) * block)], ws)
    landed(hub_all.at[pl.ds(0, MEM - 1)], h1s)
    landed(hubs.at[pl.ds(0, EV - 1)], h2s)
    result.wait()


def vm(*shape, dtype=BF):
    return pltpu.VMEM(shape, dtype)


def path(slots, width):
    near = (XS, EV, ZS * slots, width)
    far = (MEM, EV * slots, width)
    return [vm(*near), vm(*near), vm(*far), vm(*far)]


def sems():
    dma = pltpu.SemaphoreType.DMA
    return [dma, dma((XS,)), dma, dma]


def local(
    memory,
    last_time,
    event_time,
    edge_features,
    update_slot,
    update_serve,
    lookup_slot,
    lookup_serve,
    neighbour_gap,
    hub_node,
    hub_choice,
    time_freq,
    time_phase,
    gru_weight,
    gru_bias,
    query_weight,
    keyval_weight,
    output_weight,
):
    nodes, width = memory.shape
    events = event_time.shape[0]
    gates = gru_bias.shape[1]
    padded = 3 * width + 256
    routed = lookup_slot.shape[1]
    near = neighbour_gap.shape[1]
    total, total_look = update_serve.shape[1], lookup_serve.shape[1]
    args = (
        memory, last_time.reshape(1, -1), event_time.reshape(1, -1), edge_features.T, update_slot.T,
        update_serve, lookup_slot.T, lookup_serve, neighbour_gap.T, hub_node.reshape(1, 1),
        hub_choice.T, time_freq.reshape(1, -1), time_phase.reshape(1, -1), gru_weight.T, gru_bias,
        query_weight, keyval_weight, output_weight,
    )
    spec = pl.BlockSpec(memory_space=pltpu.VMEM)
    left = pl.BlockSpec(memory_space=pl.ANY)
    large = (memory, gru_weight.T, query_weight, keyval_weight, output_weight)
    dma = pltpu.SemaphoreType.DMA
    return tuple(pl.pallas_call(
        step_kernel,
        out_shape=[
            jax.ShapeDtypeStruct((nodes, width), BF),
            jax.ShapeDtypeStruct((events, width), BF),
        ],
        in_specs=[left if i in (0, 13, 15, 16, 17) else spec for i in range(len(args))],
        out_specs=[left, spec],
        scratch_shapes=path(CAP, width) + path(CAP, width) + path(1, 128) + path(CAPN, width)
        + [
            vm(gates // EV, padded),
            vm(gates, padded),
            vm(2 * events, total),
            vm(nodes, total),
            vm(nodes, gates, dtype=F32),
            vm(nodes, gates, dtype=F32),
            vm(width // 128, 128),
            vm(MEM, width // 128, 128),
            vm(MEM, width),
            vm(EV, MEM, width),
            vm(near, events, keyval_weight.shape[1], dtype=F32),
            vm(near - routed + 1, events, keyval_weight.shape[1]),
            vm(16, query_weight.shape[1], dtype=F32),
            vm(routed * events, total_look),
            vm(total_look, nodes),
            vm(XS, total // XS, total),
        ]
        + [vm(*a.shape) for a in large] + [vm(nodes, width)]
        + sems() * 4 + [dma] * 8 + [dma((len(large),)), dma],
        compiler_params=pltpu.CompilerParams(
            collective_id=0, has_side_effects=True, vmem_limit_bytes=62 << 20
        ),
    )(*args))


def solution(mesh):
    both = ("ev", "mem")
    rows, flat = P(both, None), P(both)
    return jax.shard_map(
        local,
        mesh=mesh,
        in_specs=(
            rows, flat, flat, rows, rows, rows, rows, rows, rows, flat, rows,
            P(), P(), P(None, "ev"), P(), P(), P(), P(),
        ),
        out_specs=(rows, rows),
        check_vma=False,
    )
```

```python
import functools

import jax
import jax.numpy as jnp
from jax import lax
from jax.experimental import pallas as pl
from jax.experimental.pallas import tpu as pltpu
from jax.sharding import PartitionSpec as P

HEADS = 2
DIGIT = 32
EV, MEM, ZS, XS = 8, 64, 16, 4
CHUNKS, PART = 8, 8
DEVICES = EV * MEM
CAP, CAPN = 2, 3
MESH = pl.DeviceIdType.MESH
BF = jnp.bfloat16
F32 = jnp.float32
I32 = jnp.int32


def dot(a, b):
    return jnp.dot(a, b, preferred_element_type=F32)


def dot_t(a, b):
    return lax.dot_general(a, b, (((1,), (1,)), ((), ())), preferred_element_type=F32)


def mask_bf(mask):
    return jnp.where(mask, 1.0, 0.0).astype(BF)


def iota(shape, dim):
    return lax.broadcasted_iota(I32, shape, dim)


def div(x, k):
    if k % 3 == 0:
        return ((x // (k // 3)) * 43691) >> 17
    return x // k


def place():
    e, m = lax.axis_index("ev"), lax.axis_index("mem")
    return e, m, m // ZS, lax.rem(m, ZS)


def greet():
    e, m, _, _ = place()
    barrier = pltpu.get_barrier_semaphore()

    def near(i, carry):
        pl.semaphore_signal(barrier, inc=1, device_id=(lax.rem(e + i, EV), m), device_id_type=MESH)
        return carry

    def far(i, carry):
        t = lax.rem(m + 1 + lax.rem(i + MEM // 2, MEM - 1), MEM)
        pl.semaphore_signal(barrier, inc=1, device_id=(e, t), device_id_type=MESH)
        return carry

    lax.fori_loop(0, MEM - 1, far, 0)
    lax.fori_loop(1, EV, near, 0)


def meet():
    pl.semaphore_wait(pltpu.get_barrier_semaphore(), EV + MEM - 2)


def landed(ref, sem):
    pltpu.make_async_copy(ref, ref, sem).wait()


def send_near(chunk, source, near, sent, came):
    e, m, _, _ = place()
    pltpu.make_async_copy(source.at[chunk, e], near.at[chunk, e], came.at[chunk]).start()

    def step(i, carry):
        t = lax.rem(e + i, EV)
        pltpu.make_async_remote_copy(
            source.at[chunk, t], near.at[chunk, e], sent, came.at[chunk],
            device_id=(t, m), device_id_type=MESH,
        ).start()
        return carry

    lax.fori_loop(1, EV, step, 0)


def reorder(slots):
    n = EV * PART * slots
    row, col = iota((n, n), 0), iota((n, n), 1)
    z, rest = div(row, EV * slots), row
    rest = row - z * (EV * slots)
    e = div(rest, slots)
    s = rest - e * slots
    return mask_bf(col == e * (PART * slots) + z * slots + s)


def send_far(chunk, slots, perm, near, staged, result, sent, came):
    e, m, _, mz = place()
    rows = EV * PART * slots
    width = near.shape[-1]
    landed(near.at[chunk], came[0].at[chunk])
    block = dot(perm, near[chunk].reshape(rows, width)).astype(BF)
    staged[pl.ds(chunk * PART, PART)] = block.reshape(PART, EV * slots, width)

    def step(i, carry):
        t = chunk * PART + lax.rem(mz + i, PART)

        @pl.when(t != m)
        def _():
            pltpu.make_async_remote_copy(
                staged.at[t], result.at[m], sent, came[1], device_id=(e, t), device_id_type=MESH
            ).start()

        return carry

    lax.fori_loop(0, PART, step, 0)


def finish_own(staged, result, came):
    _, m, _, _ = place()
    pltpu.make_async_copy(staged.at[m], result.at[m], came).start()


def drain(source, result, sent_near, sent_far):
    for c in range(CHUNKS):
        landed(source.at[c, pl.ds(0, EV - 1)], sent_near)
    landed(result.at[pl.ds(0, MEM - 1)], sent_far)


def column(row):
    eye = iota((128, 128), 0) == iota((128, 128), 1)
    parts = []
    for b in range(row.shape[1] // 128):
        piece = row[:, b * 128 : b * 128 + 128].astype(F32)
        parts.append(jnp.sum(jnp.where(eye, piece, 0.0), axis=1, keepdims=True))
    return jnp.concatenate(parts, axis=0).astype(I32)


def arrival(slot, cap):
    device = div(slot, cap)
    at = slot - device * cap
    return (device % MEM) * (EV * cap) + (device // MEM) * cap + at


def spread(rows, slots):
    return rows.reshape(EV, CHUNKS, PART * slots, rows.shape[1])


def encode(gap, freq, phase):
    return jnp.cos(gap.astype(F32) * freq + phase).astype(BF)


def step_kernel(
    memory_in, last_time, event_time, edge, update_slot, update_serve, lookup_slot, lookup_serve,
    neighbour_gap, hub_node, hub_choice, freq, phase, weight_in, bias, query_weight_in, keyval_weight_in,
    output_weight_in,
    new_memory_out, embedding,
    xf, nf, sf, rf, xm, nm, sm, rm, xe, ne, se, tails, xl, nl, sl, looked,
    shard, weights, gather, matches, pre_in, pre_hid, hub_one, hub_all, hub_rows, hubs, keyenc, keyhub,
    query_enc, gather_look, serve_look, route, memory, weight, query_weight, keyval_weight,
    output_weight, new_memory,
    f1s, f1r, f2s, f2r, e1s, e1r, e2s, e2r, m1s, m1r, m2s, m2r, l1s, l1r, l2s, l2r,
    ws, wr, cs, cr, h1s, h1r, h2s, h2r, load, store,
):
    e, m, mx, mz = place()
    nodes, width = memory.shape
    events = event_time.shape[1]
    edges = edge.shape[0]
    times = freq.shape[1]
    total = MEM * EV * CAP
    total_look = MEM * EV * CAPN
    order = [
        lax.rem(mx + dx, XS) * 2 + lax.rem(mz // PART + half, 2) for dx in (2, 1, 3, 0) for half in (1, 0)
    ]

    greet()
    loads = [
        pltpu.make_async_copy(a, b, load.at[i])
        for i, (a, b) in enumerate([
            (memory_in, memory), (weight_in, weight), (query_weight_in, query_weight),
            (keyval_weight_in, keyval_weight), (output_weight_in, output_weight),
        ])
    ]
    for copy in loads:
        copy.start()
    pick = column(update_serve[...]) == iota((total, nodes), 1)
    loads[0].wait()
    rows = spread(dot(mask_bf(pick), memory[...]).astype(BF), CAP)
    for c in range(CHUNKS):
        xf[c] = rows[:, c]
    meet()
    for chunk in order:
        send_near(chunk, xf, nf, f1s, f1r)

    when = event_time[...]
    late = when // DIGIT
    packed = jnp.concatenate(
        [edge[...].astype(F32), late.astype(F32), (when - late * DIGIT).astype(F32),
         jnp.zeros((64 - edges - 2, events), F32)], axis=0
    )
    extra = jnp.concatenate([packed, packed], axis=0).T.astype(BF)
    slots = update_slot[...]
    target = iota((total // CAP, events), 0) * CAP
    tail = [
        dot(mask_bf((target + s == slots[0:1]) | (target + s == slots[1:2])), extra) for s in range(CAP)
    ]
    tail = jnp.where(iota(tail[0].shape, 1) < 64, tail[0], tail[1]).astype(BF)
    tail = spread(tail, 1)
    for c in range(CHUNKS):
        xe[c] = tail[:, c]
    for chunk in order:
        send_near(chunk, xe, ne, e1s, e1r)

    loads[1].wait()
    shard[:, 0 : 2 * width] = weight[:, 0 : 2 * width]
    rest = weight.shape[1] - 2 * width
    row, col = iota((rest, width + 256), 0), iota((rest, width + 256), 1)
    source = jnp.where(
        col < width, col + times + edges,
        jnp.where(col < width + 128, jnp.where(col < width + times, col - width, -1),
                  jnp.where(col < width + 128 + edges, col - width - 128 + times, -1)))
    shard[:, 2 * width :] = dot(weight[:, 2 * width :], mask_bf(row == source)).astype(BF)
    block = shard.shape[0]

    def part(index):
        return weights.at[pl.ds(pl.multiple_of(index * block, block), block)]

    own = pltpu.make_async_copy(shard, part(e), cs)
    own.start()
    for hop in range(1, EV // 2):
        pltpu.make_async_remote_copy(
            shard, part(e), ws, wr,
            device_id=(lax.rem(e + 2 * hop, EV), m), device_id_type=MESH,
        ).start()

    perm = reorder(CAP)
    perm_one = reorder(1)
    for chunk in order:
        send_far(chunk, CAP, perm, nf, sf, rf, f2s, (f1r, f2r))
    for chunk in order:
        send_far(chunk, 1, perm_one, ne, se, tails, e2s, (e1r, e2r))
    finish_own(sf, rf, f2r)
    finish_own(se, tails, e2r)

    places = arrival(slots, CAP)
    places = column(jnp.concatenate([places[1:2], places[0:1]], axis=1))
    gather[...] = mask_bf(places == iota((2 * events, total), 1))
    slot_row = jnp.concatenate([slots[0:1], slots[1:2]], axis=1)
    for c in range(CHUNKS):
        target = iota((EV * PART * CAP, 1), 0)
        target = (target // (PART * CAP)) * (MEM * CAP) + c * (PART * CAP) + target % (PART * CAP)
        route[c] = dot(mask_bf(target == slot_row), gather[...]).astype(BF)
    serve = jnp.broadcast_to(update_serve[...].astype(F32), (16, total)).astype(BF)
    row, col = iota((total, total), 0), iota((total, total), 1)
    col = ((col // CAP) % EV) * (MEM * CAP) + (col // (CAP * EV)) * CAP + col % CAP
    serve_in = dot(serve, mask_bf(row == col))[0:1].astype(I32)
    met = serve_in == iota((nodes, total), 0)
    matches[...] = mask_bf(met)
    counts = jnp.sum(jnp.where(met, 1.0, 0.0), axis=1, keepdims=True)
    share = jnp.maximum(counts, 1.0)
    row, col = iota((total, total // CAP), 0), iota((total, total // CAP), 1)
    col = (col % EV) * (MEM * CAP) + (col // EV) * CAP
    serve_of = [dot(serve, mask_bf(row == col + s))[0:1].astype(I32) for s in range(CAP)]

    landed(weights.at[pl.ds(0, (EV // 2 - 1) * block)], wr)
    own.wait()
    partner = e + 1 - 2 * lax.rem(e, 2)
    for hop in range(EV // 2):
        index = lax.rem(e + 2 * hop, EV)
        pltpu.make_async_remote_copy(
            part(index), part(index), ws, cr, device_id=(partner, m), device_id_type=MESH
        ).start()

    landed(rf, f2r)
    for chunk in order:
        message = dot(route[chunk], rf[...].reshape(total, width)).astype(BF)
        xm[chunk] = message.reshape(EV, PART * CAP, width)
        send_near(chunk, xm, nm, m1s, m1r)
    for chunk in order:
        send_far(chunk, CAP, perm, nm, sm, rm, m2s, (m1r, m2r))
    finish_own(sm, rm, m2r)

    landed(weights.at[pl.ds(0, EV // 2 * block)], cr)
    landed(tails, e2r)
    arrived = tails[...].reshape(total // CAP, 128)
    encoded_sum, edge_sum = 0.0, []
    for s in range(CAP):
        hits = serve_of[s] == iota((nodes, total // CAP), 0)
        mine = column(serve_of[s]) == iota((total // CAP, nodes), 1)
        before = jnp.sum(jnp.where(mine, last_time[...].astype(F32), 0.0), axis=1, keepdims=True)
        digits = arrived[:, s * 64 : s * 64 + 64].astype(F32)
        time = digits[:, edges : edges + 1] * DIGIT + digits[:, edges + 1 : edges + 2]
        encoded = jnp.cos((time - before) * freq[...] + phase[...]).astype(BF)
        encoded_sum = encoded_sum + dot(mask_bf(hits), encoded)
        edge_sum.append(dot(mask_bf(hits), arrived))
    edge_sum = edge_sum[0] + pltpu.roll(edge_sum[1], 64, 1)
    encoded_mean = (encoded_sum / share).astype(BF)
    edge_mean = (edge_sum / share).astype(BF)
    w = 3 * width
    for t in range(3):
        third = pl.ds(t * width, width)
        pre_in[:, third] = (
            dot_t(memory[...], weights[third, 0:width])
            + dot_t(encoded_mean, weights[third, w : w + times])
            + dot_t(edge_mean, weights[third, w + 128 : w + 256])
            + bias[0:1, third]
        )
        pre_hid[:, third] = dot_t(memory[...], weights[third, 2 * width : 3 * width]) + bias[1:2, third]
    picks = spread(mask_bf(column(lookup_serve[...]) == iota((total_look, nodes), 1)), CAPN)
    for c in range(CHUNKS):
        serve_look[c] = picks[:, c].reshape(total_look // CHUNKS, nodes)
    perm = reorder(CAPN)

    landed(rm, m2r)
    summed = dot(matches[...], rm[...].reshape(total, width))
    averaged = (summed / share).astype(BF)

    def pre(t):
        third = pl.ds(t * width, width)
        return pre_in[:, third] + dot_t(averaged, weights[third, width : 2 * width])

    reset = jax.nn.sigmoid(pre(0) + pre_hid[:, 0:width])
    update = jax.nn.sigmoid(pre(1) + pre_hid[:, width : 2 * width])
    candidate = jnp.tanh(pre(2) + reset * pre_hid[:, 2 * width : 3 * width])
    previous = memory[...].astype(F32)
    fresh = (1.0 - update) * candidate + update * previous
    new_memory[...] = jnp.where(counts > 0, fresh, previous).astype(BF)

    for chunk in order:
        rows = dot(serve_look[chunk], new_memory[...]).astype(BF)
        xl[chunk] = rows.reshape(EV, PART * CAPN, width)
        send_near(chunk, xl, nl, l1s, l1r)
    result = pltpu.make_async_copy(new_memory, new_memory_out, store)
    result.start()
    hub = dot(mask_bf(hub_node[0] == iota((16, nodes), 1)), new_memory[...])
    hub_one[...] = jnp.concatenate(
        [hub[0:1, j * 128 : j * 128 + 128] for j in range(width // 128)], axis=0
    ).astype(BF)
    pltpu.make_async_copy(hub_one, hub_all.at[m], h1r).start()

    def hub_far(i, carry):
        t = lax.rem(m + i, MEM)
        pltpu.make_async_remote_copy(
            hub_one, hub_all.at[m], h1s, h1r, device_id=(e, t), device_id_type=MESH
        ).start()
        return carry

    lax.fori_loop(1, MEM, hub_far, 0)
    for chunk in order:
        send_far(chunk, CAPN, perm, nl, sl, looked, l2s, (l1r, l2r))
    finish_own(sl, looked, l2r)
    landed(hub_all, h1r)
    gathered = hub_all[...].astype(F32)
    hub_rows[...] = jnp.concatenate(
        [gathered[:, j, :] for j in range(width // 128)], axis=1
    ).astype(BF)
    pltpu.make_async_copy(hub_rows, hubs.at[e], h2r).start()

    def hub_near(i, carry):
        pltpu.make_async_remote_copy(
            hub_rows, hubs.at[e], h2s, h2r, device_id=(lax.rem(e + i, EV), m), device_id_type=MESH
        ).start()
        return carry

    lax.fori_loop(1, EV, hub_near, 0)

    routed = lookup_slot.shape[0]
    near = neighbour_gap.shape[0]
    for copy in loads[2:]:
        copy.wait()
    for k in range(near):
        encoded = encode(column(neighbour_gap[k : k + 1]), freq[...], phase[...])
        keyenc[k] = dot(encoded, keyval_weight[width : width + times])
    still = jnp.broadcast_to(jnp.cos(phase[...]), (16, times)).astype(BF)
    query_enc[...] = dot(still, query_weight[width : width + times])
    for k in range(routed):
        at = column(arrival(lookup_slot[k : k + 1], CAPN))
        gather_look[pl.ds(k * events, events)] = mask_bf(at == iota((events, total_look), 1))
    landed(hubs, h2r)
    for k in range(near - routed + 1):
        choice = column(hub_choice[k : k + 1])
        rows = dot(mask_bf(choice == iota((events, DEVICES), 1)), hubs[...].reshape(DEVICES, width)).astype(BF)
        keyhub[k] = (dot(rows, keyval_weight[0:width]) + keyenc[routed - 1 + k]).astype(BF)

    landed(looked, l2r)
    everything = looked[...].reshape(total_look, width)
    own_row = dot(gather_look[0:events], everything).astype(BF)
    query = (dot(own_row, query_weight[0:width]) + query_enc[0:1]).astype(BF).astype(F32)
    att = query.shape[1]
    head = att // HEADS
    keyval = []
    for k in range(near):
        if k < routed - 1:
            rows = dot(gather_look[pl.ds((k + 1) * events, events)], everything).astype(BF)
            keyval.append((dot(rows, keyval_weight[0:width]) + keyenc[k]).astype(BF))
        else:
            keyval.append(keyhub[k - routed + 1])
    mixed = []
    for h in range(HEADS):
        q = query[:, h * head : h * head + head]
        scores = [
            jnp.sum(q * kv[:, h * head : h * head + head].astype(F32), axis=1, keepdims=True)
            * head ** (-0.5)
            for kv in keyval
        ]
        top = functools.reduce(jnp.maximum, scores)
        expo = [jnp.exp(x - top) for x in scores]
        base = functools.reduce(jnp.add, expo)
        acc = 0.0
        for x, kv in zip(expo, keyval):
            prob = (x / base).astype(BF).astype(F32)
            acc = acc + prob * kv[:, att + h * head : att + h * head + head].astype(F32)
        mixed.append(acc.astype(BF))
    mixed = jnp.concatenate(mixed, axis=1)
    embedding[...] = (
        dot(mixed, output_weight[0:att]) + dot(own_row, output_weight[att : att + width])
    ).astype(BF)

    drain(xf, rf, f1s, f2s)
    drain(xe, tails, e1s, e2s)
    drain(xm, rm, m1s, m2s)
    drain(xl, looked, l1s, l2s)
    landed(weights.at[pl.ds(0, (EV - 1) * block)], ws)
    landed(hub_all.at[pl.ds(0, MEM - 1)], h1s)
    landed(hubs.at[pl.ds(0, EV - 1)], h2s)
    result.wait()


def vm(*shape, dtype=BF):
    return pltpu.VMEM(shape, dtype)


def path(slots, width):
    near = (CHUNKS, EV, PART * slots, width)
    far = (MEM, EV * slots, width)
    return [vm(*near), vm(*near), vm(*far), vm(*far)]


def sems():
    dma = pltpu.SemaphoreType.DMA
    return [dma, dma((CHUNKS,)), dma, dma]


def local(
    memory,
    last_time,
    event_time,
    edge_features,
    update_slot,
    update_serve,
    lookup_slot,
    lookup_serve,
    neighbour_gap,
    hub_node,
    hub_choice,
    time_freq,
    time_phase,
    gru_weight,
    gru_bias,
    query_weight,
    keyval_weight,
    output_weight,
):
    nodes, width = memory.shape
    events = event_time.shape[0]
    gates = gru_bias.shape[1]
    padded = 3 * width + 256
    routed = lookup_slot.shape[1]
    near = neighbour_gap.shape[1]
    total, total_look = update_serve.shape[1], lookup_serve.shape[1]
    args = (
        memory, last_time.reshape(1, -1), event_time.reshape(1, -1), edge_features.T, update_slot.T,
        update_serve, lookup_slot.T, lookup_serve, neighbour_gap.T, hub_node,
        hub_choice.T, time_freq.reshape(1, -1), time_phase.reshape(1, -1), gru_weight.T, gru_bias,
        query_weight, keyval_weight, output_weight,
    )
    spec = pl.BlockSpec(memory_space=pltpu.VMEM)
    left = pl.BlockSpec(memory_space=pl.ANY)
    scalar = pl.BlockSpec(memory_space=pltpu.SMEM)
    large = (memory, gru_weight.T, query_weight, keyval_weight, output_weight)
    dma = pltpu.SemaphoreType.DMA
    return tuple(pl.pallas_call(
        step_kernel,
        out_shape=[
            jax.ShapeDtypeStruct((nodes, width), BF),
            jax.ShapeDtypeStruct((events, width), BF),
        ],
        in_specs=[
            left if i in (0, 13, 15, 16, 17) else scalar if i == 9 else spec for i in range(len(args))
        ],
        out_specs=[left, spec],
        scratch_shapes=path(CAP, width) + path(CAP, width) + path(1, 128) + path(CAPN, width)
        + [
            vm(gates // EV, padded),
            vm(gates, padded),
            vm(2 * events, total),
            vm(nodes, total),
            vm(nodes, gates, dtype=F32),
            vm(nodes, gates, dtype=F32),
            vm(width // 128, 128),
            vm(MEM, width // 128, 128),
            vm(MEM, width),
            vm(EV, MEM, width),
            vm(near, events, keyval_weight.shape[1], dtype=F32),
            vm(near - routed + 1, events, keyval_weight.shape[1]),
            vm(16, query_weight.shape[1], dtype=F32),
            vm(routed * events, total_look),
            vm(CHUNKS, total_look // CHUNKS, nodes),
            vm(CHUNKS, total // CHUNKS, total),
        ]
        + [vm(*a.shape) for a in large] + [vm(nodes, width)]
        + sems() * 4 + [dma] * 8 + [dma((len(large),)), dma],
        compiler_params=pltpu.CompilerParams(
            collective_id=0, has_side_effects=True, vmem_limit_bytes=62 << 20
        ),
    )(*args))


def solution(mesh):
    both = ("ev", "mem")
    rows, flat = P(both, None), P(both)
    return jax.shard_map(
        local,
        mesh=mesh,
        in_specs=(
            rows, flat, flat, rows, rows, rows, rows, rows, rows, flat, rows,
            P(), P(), P(None, "ev"), P(), P(), P(), P(),
        ),
        out_specs=(rows, rows),
        check_vma=False,
    )
```

```python
import functools

import jax
import jax.numpy as jnp
from jax import lax
from jax.experimental import pallas as pl
from jax.experimental.pallas import tpu as pltpu
from jax.sharding import PartitionSpec as P

HEADS = 2
DIGIT = 32
EV, MEM, ZS, XS = 8, 64, 16, 4
CHUNKS, PART = 8, 8
DEVICES = EV * MEM
CAP, CAPN = 2, 3
MESH = pl.DeviceIdType.MESH
BF = jnp.bfloat16
F32 = jnp.float32
I32 = jnp.int32


def dot(a, b):
    return jnp.dot(a, b, preferred_element_type=F32)


def dot_t(a, b):
    return lax.dot_general(a, b, (((1,), (1,)), ((), ())), preferred_element_type=F32)


def mask_bf(mask):
    return jnp.where(mask, 1.0, 0.0).astype(BF)


def iota(shape, dim):
    return lax.broadcasted_iota(I32, shape, dim)


def div(x, k):
    if k % 3 == 0:
        return ((x // (k // 3)) * 43691) >> 17
    return x // k


def place():
    e, m = lax.axis_index("ev"), lax.axis_index("mem")
    return e, m, m // ZS, lax.rem(m, ZS)


def greet():
    e, m, _, _ = place()
    barrier = pltpu.get_barrier_semaphore()

    def near(i, carry):
        pl.semaphore_signal(barrier, inc=1, device_id=(lax.rem(e + i, EV), m), device_id_type=MESH)
        return carry

    def far(i, carry):
        t = lax.rem(m + 1 + lax.rem(i + MEM // 2, MEM - 1), MEM)
        pl.semaphore_signal(barrier, inc=1, device_id=(e, t), device_id_type=MESH)
        return carry

    lax.fori_loop(0, MEM - 1, far, 0)
    lax.fori_loop(1, EV, near, 0)


def meet():
    pl.semaphore_wait(pltpu.get_barrier_semaphore(), EV + MEM - 2)


def landed(ref, sem):
    pltpu.make_async_copy(ref, ref, sem).wait()


def send_near(chunk, source, near, sent, came):
    e, m, _, _ = place()
    pltpu.make_async_copy(source.at[chunk, e], near.at[chunk, e], came.at[chunk]).start()

    def step(i, carry):
        t = lax.rem(e + i, EV)
        pltpu.make_async_remote_copy(
            source.at[chunk, t], near.at[chunk, e], sent, came.at[chunk],
            device_id=(t, m), device_id_type=MESH,
        ).start()
        return carry

    lax.fori_loop(1, EV, step, 0)


def reorder(slots):
    n = EV * PART * slots
    row, col = iota((n, n), 0), iota((n, n), 1)
    z, rest = div(row, EV * slots), row
    rest = row - z * (EV * slots)
    e = div(rest, slots)
    s = rest - e * slots
    return mask_bf(col == e * (PART * slots) + z * slots + s)


def send_far(chunk, slots, perm, near, staged, result, sent, came):
    e, m, _, mz = place()
    rows = EV * PART * slots
    width = near.shape[-1]
    landed(near.at[chunk], came[0].at[chunk])
    block = dot(perm, near[chunk].reshape(rows, width)).astype(BF)
    staged[pl.ds(chunk * PART, PART)] = block.reshape(PART, EV * slots, width)

    def step(i, carry):
        t = chunk * PART + lax.rem(mz + i, PART)

        @pl.when(t != m)
        def _():
            pltpu.make_async_remote_copy(
                staged.at[t], result.at[m], sent, came[1], device_id=(e, t), device_id_type=MESH
            ).start()

        return carry

    lax.fori_loop(0, PART, step, 0)


def finish_own(staged, result, came):
    _, m, _, _ = place()
    pltpu.make_async_copy(staged.at[m], result.at[m], came).start()


def drain(source, result, sent_near, sent_far):
    for c in range(CHUNKS):
        landed(source.at[c, pl.ds(0, EV - 1)], sent_near)
    landed(result.at[pl.ds(0, MEM - 1)], sent_far)


def column(row):
    eye = iota((128, 128), 0) == iota((128, 128), 1)
    parts = []
    for b in range(row.shape[1] // 128):
        piece = row[:, b * 128 : b * 128 + 128].astype(F32)
        parts.append(jnp.sum(jnp.where(eye, piece, 0.0), axis=1, keepdims=True))
    return jnp.concatenate(parts, axis=0).astype(I32)


def arrival(slot, cap):
    device = div(slot, cap)
    at = slot - device * cap
    return (device % MEM) * (EV * cap) + (device // MEM) * cap + at


def spread(rows, slots):
    return rows.reshape(EV, CHUNKS, PART * slots, rows.shape[1])


def encode(gap, freq, phase):
    return jnp.cos(gap.astype(F32) * freq + phase).astype(BF)


def step_kernel(
    update_serve_in, memory_in, event_time_in, edge_in, update_slot_in, weight_in, last_time_in,
    lookup_slot_in, lookup_serve_in, neighbour_gap_in, hub_choice_in, freq_in, phase_in, bias_in,
    query_weight_in, keyval_weight_in, output_weight_in, hub_node,
    new_memory_out, embedding,
    xf, nf, sf, rf, xm, nm, sm, rm, xe, ne, se, tails, xl, nl, sl, looked,
    shard, weights, gather, matches, pre_in, pre_hid, hub_one, hub_all, hub_rows, hubs, keyenc, keyhub,
    query_enc, gather_look, serve_look, route, new_memory,
    update_serve, memory, event_time, edge, update_slot, weight, last_time, lookup_slot, lookup_serve,
    neighbour_gap, hub_choice, freq, phase, bias, query_weight, keyval_weight, output_weight,
    f1s, f1r, f2s, f2r, e1s, e1r, e2s, e2r, m1s, m1r, m2s, m2r, l1s, l1r, l2s, l2r,
    ws, wr, cs, cr, h1s, h1r, hxs, hxr, h2s, h2r, load, store,
):
    e, m, mx, mz = place()
    nodes, width = memory.shape
    events = event_time.shape[1]
    edges = edge.shape[0]
    times = freq.shape[1]
    total = MEM * EV * CAP
    total_look = MEM * EV * CAPN
    order = [
        lax.rem(mx + dx, XS) * 2 + lax.rem(mz // PART + half, 2) for dx in (2, 1, 3, 0) for half in (1, 0)
    ]

    greet()
    loads = [
        pltpu.make_async_copy(a, b, load.at[i])
        for i, (a, b) in enumerate([
            (update_serve_in, update_serve), (memory_in, memory), (event_time_in, event_time),
            (edge_in, edge), (update_slot_in, update_slot), (weight_in, weight), (last_time_in, last_time),
            (lookup_slot_in, lookup_slot), (lookup_serve_in, lookup_serve),
            (neighbour_gap_in, neighbour_gap), (hub_choice_in, hub_choice), (freq_in, freq),
            (phase_in, phase), (bias_in, bias), (query_weight_in, query_weight),
            (keyval_weight_in, keyval_weight), (output_weight_in, output_weight),
        ])
    ]
    for copy in loads:
        copy.start()
    loads[0].wait()
    pick = column(update_serve[...]) == iota((total, nodes), 1)
    loads[1].wait()
    rows = spread(dot(mask_bf(pick), memory[...]).astype(BF), CAP)
    for c in range(CHUNKS):
        xf[c] = rows[:, c]
    meet()
    for chunk in order:
        send_near(chunk, xf, nf, f1s, f1r)

    for copy in loads[2:5]:
        copy.wait()
    when = event_time[...]
    late = when // DIGIT
    packed = jnp.concatenate(
        [edge[...].astype(F32), late.astype(F32), (when - late * DIGIT).astype(F32),
         jnp.zeros((64 - edges - 2, events), F32)], axis=0
    )
    extra = jnp.concatenate([packed, packed], axis=0).T.astype(BF)
    slots = update_slot[...]
    target = iota((total // CAP, events), 0) * CAP
    tail = [
        dot(mask_bf((target + s == slots[0:1]) | (target + s == slots[1:2])), extra) for s in range(CAP)
    ]
    tail = jnp.where(iota(tail[0].shape, 1) < 64, tail[0], tail[1]).astype(BF)
    tail = spread(tail, 1)
    for c in range(CHUNKS):
        xe[c] = tail[:, c]
    for chunk in order:
        send_near(chunk, xe, ne, e1s, e1r)

    for copy in loads[5:]:
        copy.wait()
    shard[:, 0 : 2 * width] = weight[:, 0 : 2 * width]
    rest = weight.shape[1] - 2 * width
    row, col = iota((rest, width + 256), 0), iota((rest, width + 256), 1)
    source = jnp.where(
        col < width, col + times + edges,
        jnp.where(col < width + 128, jnp.where(col < width + times, col - width, -1),
                  jnp.where(col < width + 128 + edges, col - width - 128 + times, -1)))
    shard[:, 2 * width :] = dot(weight[:, 2 * width :], mask_bf(row == source)).astype(BF)
    block = shard.shape[0]

    def part(index):
        return weights.at[pl.ds(pl.multiple_of(index * block, block), block)]

    own = pltpu.make_async_copy(shard, part(e), cs)
    own.start()
    for hop in range(1, EV // 2):
        pltpu.make_async_remote_copy(
            shard, part(e), ws, wr,
            device_id=(lax.rem(e + 2 * hop, EV), m), device_id_type=MESH,
        ).start()

    perm = reorder(CAP)
    perm_one = reorder(1)
    for chunk in order:
        send_far(chunk, CAP, perm, nf, sf, rf, f2s, (f1r, f2r))
    for chunk in order:
        send_far(chunk, 1, perm_one, ne, se, tails, e2s, (e1r, e2r))
    finish_own(sf, rf, f2r)
    finish_own(se, tails, e2r)

    places = arrival(slots, CAP)
    places = column(jnp.concatenate([places[1:2], places[0:1]], axis=1))
    gather[...] = mask_bf(places == iota((2 * events, total), 1))
    slot_row = jnp.concatenate([slots[0:1], slots[1:2]], axis=1)
    for c in range(CHUNKS):
        target = iota((EV * PART * CAP, 1), 0)
        target = (target // (PART * CAP)) * (MEM * CAP) + c * (PART * CAP) + target % (PART * CAP)
        route[c] = dot(mask_bf(target == slot_row), gather[...]).astype(BF)
    serve = jnp.broadcast_to(update_serve[...].astype(F32), (16, total)).astype(BF)
    row, col = iota((total, total), 0), iota((total, total), 1)
    col = ((col // CAP) % EV) * (MEM * CAP) + (col // (CAP * EV)) * CAP + col % CAP
    serve_in = dot(serve, mask_bf(row == col))[0:1].astype(I32)
    met = serve_in == iota((nodes, total), 0)
    matches[...] = mask_bf(met)
    counts = jnp.sum(jnp.where(met, 1.0, 0.0), axis=1, keepdims=True)
    share = jnp.maximum(counts, 1.0)
    row, col = iota((total, total // CAP), 0), iota((total, total // CAP), 1)
    col = (col % EV) * (MEM * CAP) + (col // EV) * CAP
    serve_of = [dot(serve, mask_bf(row == col + s))[0:1].astype(I32) for s in range(CAP)]

    landed(weights.at[pl.ds(0, (EV // 2 - 1) * block)], wr)
    own.wait()
    partner = e + 1 - 2 * lax.rem(e, 2)
    for hop in range(EV // 2):
        index = lax.rem(e + 2 * hop, EV)
        pltpu.make_async_remote_copy(
            part(index), part(index), ws, cr, device_id=(partner, m), device_id_type=MESH
        ).start()

    landed(rf, f2r)
    for chunk in order:
        message = dot(route[chunk], rf[...].reshape(total, width)).astype(BF)
        xm[chunk] = message.reshape(EV, PART * CAP, width)
        send_near(chunk, xm, nm, m1s, m1r)
    for chunk in order:
        send_far(chunk, CAP, perm, nm, sm, rm, m2s, (m1r, m2r))
    finish_own(sm, rm, m2r)

    landed(weights.at[pl.ds(0, EV // 2 * block)], cr)
    landed(tails, e2r)
    arrived = tails[...].reshape(total // CAP, 128)
    encoded_sum, edge_sum = 0.0, []
    for s in range(CAP):
        hits = serve_of[s] == iota((nodes, total // CAP), 0)
        mine = column(serve_of[s]) == iota((total // CAP, nodes), 1)
        before = jnp.sum(jnp.where(mine, last_time[...].astype(F32), 0.0), axis=1, keepdims=True)
        digits = arrived[:, s * 64 : s * 64 + 64].astype(F32)
        time = digits[:, edges : edges + 1] * DIGIT + digits[:, edges + 1 : edges + 2]
        encoded = jnp.cos((time - before) * freq[...] + phase[...]).astype(BF)
        encoded_sum = encoded_sum + dot(mask_bf(hits), encoded)
        edge_sum.append(dot(mask_bf(hits), arrived))
    edge_sum = edge_sum[0] + pltpu.roll(edge_sum[1], 64, 1)
    encoded_mean = (encoded_sum / share).astype(BF)
    edge_mean = (edge_sum / share).astype(BF)
    w = 3 * width
    for t in range(3):
        third = pl.ds(t * width, width)
        pre_in[:, third] = (
            dot_t(memory[...], weights[third, 0:width])
            + dot_t(encoded_mean, weights[third, w : w + times])
            + dot_t(edge_mean, weights[third, w + 128 : w + 256])
            + bias[0:1, third]
        )
        pre_hid[:, third] = dot_t(memory[...], weights[third, 2 * width : 3 * width]) + bias[1:2, third]
    picks = spread(mask_bf(column(lookup_serve[...]) == iota((total_look, nodes), 1)), CAPN)
    for c in range(CHUNKS):
        serve_look[c] = picks[:, c].reshape(total_look // CHUNKS, nodes)
    perm = reorder(CAPN)

    landed(rm, m2r)
    summed = dot(matches[...], rm[...].reshape(total, width))
    averaged = (summed / share).astype(BF)

    def pre(t):
        third = pl.ds(t * width, width)
        return pre_in[:, third] + dot_t(averaged, weights[third, width : 2 * width])

    reset = jax.nn.sigmoid(pre(0) + pre_hid[:, 0:width])
    update = jax.nn.sigmoid(pre(1) + pre_hid[:, width : 2 * width])
    candidate = jnp.tanh(pre(2) + reset * pre_hid[:, 2 * width : 3 * width])
    previous = memory[...].astype(F32)
    fresh = (1.0 - update) * candidate + update * previous
    new_memory[...] = jnp.where(counts > 0, fresh, previous).astype(BF)

    for chunk in order:
        rows = dot(serve_look[chunk], new_memory[...]).astype(BF)
        xl[chunk] = rows.reshape(EV, PART * CAPN, width)
        send_near(chunk, xl, nl, l1s, l1r)
    result = pltpu.make_async_copy(new_memory, new_memory_out, store)
    result.start()
    hub = dot(mask_bf(hub_node[0] == iota((16, nodes), 1)), new_memory[...])
    hub_one[...] = jnp.concatenate(
        [hub[0:1, j * 128 : j * 128 + 128] for j in range(width // 128)], axis=0
    ).astype(BF)
    pltpu.make_async_copy(hub_one, hub_all.at[m], h1r).start()

    def hub_far(i, carry):
        t = mx * ZS + lax.rem(mz + i, ZS)
        pltpu.make_async_remote_copy(
            hub_one, hub_all.at[m], h1s, h1r, device_id=(e, t), device_id_type=MESH
        ).start()
        return carry

    lax.fori_loop(1, ZS, hub_far, 0)
    for chunk in order:
        send_far(chunk, CAPN, perm, nl, sl, looked, l2s, (l1r, l2r))
    finish_own(sl, looked, l2r)
    line = hub_all.at[pl.ds(mx * ZS, ZS)]
    landed(line, h1r)
    for dx in range(1, XS):
        pltpu.make_async_remote_copy(
            line, line, hxs, hxr, device_id=(e, lax.rem(mx + dx, XS) * ZS + mz), device_id_type=MESH
        ).start()
    landed(hub_all.at[pl.ds(0, (XS - 1) * ZS)], hxr)
    gathered = hub_all[...].astype(F32)
    hub_rows[...] = jnp.concatenate(
        [gathered[:, j, :] for j in range(width // 128)], axis=1
    ).astype(BF)
    pltpu.make_async_copy(hub_rows, hubs.at[e], h2r).start()

    def hub_near(i, carry):
        pltpu.make_async_remote_copy(
            hub_rows, hubs.at[e], h2s, h2r, device_id=(lax.rem(e + i, EV), m), device_id_type=MESH
        ).start()
        return carry

    lax.fori_loop(1, EV, hub_near, 0)

    routed = lookup_slot.shape[0]
    near = neighbour_gap.shape[0]
    for k in range(near):
        encoded = encode(column(neighbour_gap[k : k + 1]), freq[...], phase[...])
        keyenc[k] = dot(encoded, keyval_weight[width : width + times])
    still = jnp.broadcast_to(jnp.cos(phase[...]), (16, times)).astype(BF)
    query_enc[...] = dot(still, query_weight[width : width + times])
    for k in range(routed):
        at = column(arrival(lookup_slot[k : k + 1], CAPN))
        gather_look[pl.ds(k * events, events)] = mask_bf(at == iota((events, total_look), 1))
    landed(hubs, h2r)
    for k in range(near - routed + 1):
        choice = column(hub_choice[k : k + 1])
        rows = dot(mask_bf(choice == iota((events, DEVICES), 1)), hubs[...].reshape(DEVICES, width)).astype(BF)
        keyhub[k] = (dot(rows, keyval_weight[0:width]) + keyenc[routed - 1 + k]).astype(BF)

    landed(looked, l2r)
    everything = looked[...].reshape(total_look, width)
    own_row = dot(gather_look[0:events], everything).astype(BF)
    query = (dot(own_row, query_weight[0:width]) + query_enc[0:1]).astype(BF).astype(F32)
    att = query.shape[1]
    head = att // HEADS
    keyval = []
    for k in range(near):
        if k < routed - 1:
            rows = dot(gather_look[pl.ds((k + 1) * events, events)], everything).astype(BF)
            keyval.append((dot(rows, keyval_weight[0:width]) + keyenc[k]).astype(BF))
        else:
            keyval.append(keyhub[k - routed + 1])
    mixed = []
    for h in range(HEADS):
        q = query[:, h * head : h * head + head]
        scores = [
            jnp.sum(q * kv[:, h * head : h * head + head].astype(F32), axis=1, keepdims=True)
            * head ** (-0.5)
            for kv in keyval
        ]
        top = functools.reduce(jnp.maximum, scores)
        expo = [jnp.exp(x - top) for x in scores]
        base = functools.reduce(jnp.add, expo)
        acc = 0.0
        for x, kv in zip(expo, keyval):
            prob = (x / base).astype(BF).astype(F32)
            acc = acc + prob * kv[:, att + h * head : att + h * head + head].astype(F32)
        mixed.append(acc.astype(BF))
    mixed = jnp.concatenate(mixed, axis=1)
    embedding[...] = (
        dot(mixed, output_weight[0:att]) + dot(own_row, output_weight[att : att + width])
    ).astype(BF)

    drain(xf, rf, f1s, f2s)
    drain(xe, tails, e1s, e2s)
    drain(xm, rm, m1s, m2s)
    drain(xl, looked, l1s, l2s)
    landed(weights.at[pl.ds(0, (EV - 1) * block)], ws)
    landed(hub_all.at[pl.ds(0, ZS - 1)], h1s)
    landed(hub_all.at[pl.ds(0, (XS - 1) * ZS)], hxs)
    landed(hubs.at[pl.ds(0, EV - 1)], h2s)
    result.wait()


def vm(*shape, dtype=BF):
    return pltpu.VMEM(shape, dtype)


def path(slots, width):
    near = (CHUNKS, EV, PART * slots, width)
    far = (MEM, EV * slots, width)
    return [vm(*near), vm(*near), vm(*far), vm(*far)]


def sems():
    dma = pltpu.SemaphoreType.DMA
    return [dma, dma((CHUNKS,)), dma, dma]


def local(
    memory,
    last_time,
    event_time,
    edge_features,
    update_slot,
    update_serve,
    lookup_slot,
    lookup_serve,
    neighbour_gap,
    hub_node,
    hub_choice,
    time_freq,
    time_phase,
    gru_weight,
    gru_bias,
    query_weight,
    keyval_weight,
    output_weight,
):
    nodes, width = memory.shape
    events = event_time.shape[0]
    gates = gru_bias.shape[1]
    padded = 3 * width + 256
    routed = lookup_slot.shape[1]
    near = neighbour_gap.shape[1]
    total, total_look = update_serve.shape[1], lookup_serve.shape[1]
    args = (
        update_serve, memory, event_time.reshape(1, -1), edge_features.T, update_slot.T, gru_weight.T,
        last_time.reshape(1, -1), lookup_slot.T, lookup_serve, neighbour_gap.T, hub_choice.T,
        time_freq.reshape(1, -1), time_phase.reshape(1, -1), gru_bias, query_weight, keyval_weight,
        output_weight,
    )
    dma = pltpu.SemaphoreType.DMA
    return tuple(pl.pallas_call(
        step_kernel,
        out_shape=[
            jax.ShapeDtypeStruct((nodes, width), BF),
            jax.ShapeDtypeStruct((events, width), BF),
        ],
        in_specs=[pl.BlockSpec(memory_space=pltpu.HBM)] * len(args)
        + [pl.BlockSpec(memory_space=pltpu.SMEM)],
        out_specs=[pl.BlockSpec(memory_space=pl.ANY), pl.BlockSpec(memory_space=pltpu.VMEM)],
        scratch_shapes=path(CAP, width) + path(CAP, width) + path(1, 128) + path(CAPN, width)
        + [
            vm(gates // EV, padded),
            vm(gates, padded),
            vm(2 * events, total),
            vm(nodes, total),
            vm(nodes, gates, dtype=F32),
            vm(nodes, gates, dtype=F32),
            vm(width // 128, 128),
            vm(MEM, width // 128, 128),
            vm(MEM, width),
            vm(EV, MEM, width),
            vm(near, events, keyval_weight.shape[1], dtype=F32),
            vm(near - routed + 1, events, keyval_weight.shape[1]),
            vm(16, query_weight.shape[1], dtype=F32),
            vm(routed * events, total_look),
            vm(CHUNKS, total_look // CHUNKS, nodes),
            vm(CHUNKS, total // CHUNKS, total),
        ]
        + [vm(nodes, width)] + [vm(*a.shape, dtype=a.dtype) for a in args]
        + sems() * 4 + [dma] * 10 + [dma((len(args),)), dma],
        compiler_params=pltpu.CompilerParams(
            collective_id=0, has_side_effects=True, vmem_limit_bytes=62 << 20
        ),
    )(*args, hub_node))


def solution(mesh):
    both = ("ev", "mem")
    rows, flat = P(both, None), P(both)
    return jax.shard_map(
        local,
        mesh=mesh,
        in_specs=(
            rows, flat, flat, rows, rows, rows, rows, rows, rows, flat, rows,
            P(), P(), P(None, "ev"), P(), P(), P(), P(),
        ),
        out_specs=(rows, rows),
        check_vma=False,
    )
```

```python
import functools

import jax
import jax.numpy as jnp
from jax import lax
from jax.experimental import pallas as pl
from jax.experimental.pallas import tpu as pltpu
from jax.sharding import PartitionSpec as P

HEADS = 2
DIGIT = 32
EV, MEM, ZS, XS = 8, 64, 16, 4
WIDE, FINE = 8, 16
DEVICES = EV * MEM
CAP, CAPN = 2, 3
MESH = pl.DeviceIdType.MESH
BF = jnp.bfloat16
F32 = jnp.float32
I32 = jnp.int32


def dot(a, b):
    return jnp.dot(a, b, preferred_element_type=F32)


def dot_t(a, b):
    return lax.dot_general(a, b, (((1,), (1,)), ((), ())), preferred_element_type=F32)


def mask_bf(mask):
    return jnp.where(mask, 1.0, 0.0).astype(BF)


def iota(shape, dim):
    return lax.broadcasted_iota(I32, shape, dim)


def div(x, k):
    if k % 3 == 0:
        return ((x // (k // 3)) * 43691) >> 17
    return x // k


def place():
    e, m = lax.axis_index("ev"), lax.axis_index("mem")
    return e, m, m // ZS, lax.rem(m, ZS)


def greet():
    e, m, _, _ = place()
    barrier = pltpu.get_barrier_semaphore()

    def near(i, carry):
        pl.semaphore_signal(barrier, inc=1, device_id=(lax.rem(e + i, EV), m), device_id_type=MESH)
        return carry

    def far(i, carry):
        t = lax.rem(m + 1 + lax.rem(i + MEM // 2, MEM - 1), MEM)
        pl.semaphore_signal(barrier, inc=1, device_id=(e, t), device_id_type=MESH)
        return carry

    lax.fori_loop(0, MEM - 1, far, 0)
    lax.fori_loop(1, EV, near, 0)


def meet():
    pl.semaphore_wait(pltpu.get_barrier_semaphore(), EV + MEM - 2)


def landed(ref, sem):
    pltpu.make_async_copy(ref, ref, sem).wait()


def send_near(chunk, source, near, sent, came):
    e, m, _, _ = place()
    pltpu.make_async_copy(source.at[chunk, e], near.at[chunk, e], came.at[chunk]).start()

    def step(i, carry):
        t = lax.rem(e + i, EV)
        pltpu.make_async_remote_copy(
            source.at[chunk, t], near.at[chunk, e], sent, came.at[chunk],
            device_id=(t, m), device_id_type=MESH,
        ).start()
        return carry

    lax.fori_loop(1, EV, step, 0)


def reorder(slots, chunks):
    part = MEM // chunks
    n = EV * part * slots
    row, col = iota((n, n), 0), iota((n, n), 1)
    z, rest = div(row, EV * slots), row
    rest = row - z * (EV * slots)
    e = div(rest, slots)
    s = rest - e * slots
    return mask_bf(col == e * (part * slots) + z * slots + s)


def send_far(chunk, slots, perm, near, staged, result, sent, came):
    e, m, _, mz = place()
    part = MEM // near.shape[0]
    rows = EV * part * slots
    width = near.shape[-1]
    landed(near.at[chunk], came[0].at[chunk])
    block = dot(perm, near[chunk].reshape(rows, width)).astype(BF)
    staged[pl.ds(chunk * part, part)] = block.reshape(part, EV * slots, width)

    def step(i, carry):
        t = chunk * part + lax.rem(mz + i, part)

        @pl.when(t != m)
        def _():
            pltpu.make_async_remote_copy(
                staged.at[t], result.at[m], sent, came[1], device_id=(e, t), device_id_type=MESH
            ).start()

        return carry

    lax.fori_loop(0, part, step, 0)


def finish_own(staged, result, came):
    _, m, _, _ = place()
    pltpu.make_async_copy(staged.at[m], result.at[m], came).start()


def drain(source, result, sent_near, sent_far):
    for c in range(source.shape[0]):
        landed(source.at[c, pl.ds(0, EV - 1)], sent_near)
    landed(result.at[pl.ds(0, MEM - 1)], sent_far)


def column(row):
    eye = iota((128, 128), 0) == iota((128, 128), 1)
    parts = []
    for b in range(row.shape[1] // 128):
        piece = row[:, b * 128 : b * 128 + 128].astype(F32)
        parts.append(jnp.sum(jnp.where(eye, piece, 0.0), axis=1, keepdims=True))
    return jnp.concatenate(parts, axis=0).astype(I32)


def arrival(slot, cap):
    device = div(slot, cap)
    at = slot - device * cap
    return (device % MEM) * (EV * cap) + (device // MEM) * cap + at


def spread(rows, slots, chunks):
    return rows.reshape(EV, chunks, MEM // chunks * slots, rows.shape[1])


def encode(gap, freq, phase):
    return jnp.cos(gap.astype(F32) * freq + phase).astype(BF)


def step_kernel(
    update_serve_in, memory_in, event_time_in, edge_in, update_slot_in, weight_in, last_time_in,
    lookup_slot_in, lookup_serve_in, neighbour_gap_in, hub_choice_in, freq_in, phase_in, bias_in,
    query_weight_in, keyval_weight_in, output_weight_in, hub_node,
    new_memory_out, embedding,
    xf, nf, sf, rf, xm, nm, sm, rm, xe, ne, se, tails, xl, nl, sl, looked,
    shard, weights, gather, matches, pre_in, pre_hid, hub_one, hub_all, hub_rows, hubs, keyenc, keyhub,
    query_enc, gather_look, serve_look, route, new_memory,
    update_serve, memory, event_time, edge, update_slot, weight, last_time, lookup_slot, lookup_serve,
    neighbour_gap, hub_choice, freq, phase, bias, query_weight, keyval_weight, output_weight,
    f1s, f1r, f2s, f2r, e1s, e1r, e2s, e2r, m1s, m1r, m2s, m2r, l1s, l1r, l2s, l2r,
    ws, wr, cs, cr, h1s, h1r, hxs, hxr, h2s, h2r, load, store,
):
    e, m, mx, mz = place()
    nodes, width = memory.shape
    events = event_time.shape[1]
    edges = edge.shape[0]
    times = freq.shape[1]
    total = MEM * EV * CAP
    total_look = MEM * EV * CAPN
    order = [
        lax.rem(mx + dx, XS) * 2 + lax.rem(mz // 8 + half, 2) for dx in (2, 1, 3, 0) for half in (1, 0)
    ]
    fine = [
        lax.rem(mx + dx, XS) * 4 + lax.rem(mz // 4 + dz, 4) for dx in (2, 1, 3, 0) for dz in (2, 1, 3, 0)
    ]

    greet()
    loads = [
        pltpu.make_async_copy(a, b, load.at[i])
        for i, (a, b) in enumerate([
            (update_serve_in, update_serve), (memory_in, memory), (event_time_in, event_time),
            (edge_in, edge), (update_slot_in, update_slot), (weight_in, weight), (last_time_in, last_time),
            (lookup_slot_in, lookup_slot), (lookup_serve_in, lookup_serve),
            (neighbour_gap_in, neighbour_gap), (hub_choice_in, hub_choice), (freq_in, freq),
            (phase_in, phase), (bias_in, bias), (query_weight_in, query_weight),
            (keyval_weight_in, keyval_weight), (output_weight_in, output_weight),
        ])
    ]
    for copy in loads:
        copy.start()
    loads[0].wait()
    pick = column(update_serve[...]) == iota((total, nodes), 1)
    loads[1].wait()
    rows = spread(dot(mask_bf(pick), memory[...]).astype(BF), CAP, FINE)
    for c in range(FINE):
        xf[c] = rows[:, c]
    meet()
    for chunk in fine:
        send_near(chunk, xf, nf, f1s, f1r)

    for copy in loads[2:5]:
        copy.wait()
    when = event_time[...]
    late = when // DIGIT
    packed = jnp.concatenate(
        [edge[...].astype(F32), late.astype(F32), (when - late * DIGIT).astype(F32),
         jnp.zeros((64 - edges - 2, events), F32)], axis=0
    )
    extra = jnp.concatenate([packed, packed], axis=0).T.astype(BF)
    slots = update_slot[...]
    target = iota((total // CAP, events), 0) * CAP
    tail = [
        dot(mask_bf((target + s == slots[0:1]) | (target + s == slots[1:2])), extra) for s in range(CAP)
    ]
    tail = jnp.where(iota(tail[0].shape, 1) < 64, tail[0], tail[1]).astype(BF)
    tail = spread(tail, 1, WIDE)
    for c in range(WIDE):
        xe[c] = tail[:, c]
    for chunk in order:
        send_near(chunk, xe, ne, e1s, e1r)

    for copy in loads[5:]:
        copy.wait()
    shard[:, 0 : 2 * width] = weight[:, 0 : 2 * width]
    rest = weight.shape[1] - 2 * width
    row, col = iota((rest, width + 256), 0), iota((rest, width + 256), 1)
    source = jnp.where(
        col < width, col + times + edges,
        jnp.where(col < width + 128, jnp.where(col < width + times, col - width, -1),
                  jnp.where(col < width + 128 + edges, col - width - 128 + times, -1)))
    shard[:, 2 * width :] = dot(weight[:, 2 * width :], mask_bf(row == source)).astype(BF)
    block = shard.shape[0]

    def part(index):
        return weights.at[pl.ds(pl.multiple_of(index * block, block), block)]

    own = pltpu.make_async_copy(shard, part(e), cs)
    own.start()
    for hop in range(1, EV // 2):
        pltpu.make_async_remote_copy(
            shard, part(e), ws, wr,
            device_id=(lax.rem(e + 2 * hop, EV), m), device_id_type=MESH,
        ).start()

    perm = reorder(CAP, FINE)
    perm_one = reorder(1, WIDE)
    for chunk in fine:
        send_far(chunk, CAP, perm, nf, sf, rf, f2s, (f1r, f2r))
    for chunk in order:
        send_far(chunk, 1, perm_one, ne, se, tails, e2s, (e1r, e2r))
    finish_own(sf, rf, f2r)
    finish_own(se, tails, e2r)

    places = arrival(slots, CAP)
    places = column(jnp.concatenate([places[1:2], places[0:1]], axis=1))
    gather[...] = mask_bf(places == iota((2 * events, total), 1))
    slot_row = jnp.concatenate([slots[0:1], slots[1:2]], axis=1)
    few = MEM // FINE
    for c in range(FINE):
        target = iota((EV * few * CAP, 1), 0)
        target = (target // (few * CAP)) * (MEM * CAP) + c * (few * CAP) + target % (few * CAP)
        route[c] = dot(mask_bf(target == slot_row), gather[...]).astype(BF)
    serve = jnp.broadcast_to(update_serve[...].astype(F32), (16, total)).astype(BF)
    row, col = iota((total, total), 0), iota((total, total), 1)
    col = ((col // CAP) % EV) * (MEM * CAP) + (col // (CAP * EV)) * CAP + col % CAP
    serve_in = dot(serve, mask_bf(row == col))[0:1].astype(I32)
    met = serve_in == iota((nodes, total), 0)
    matches[...] = mask_bf(met)
    counts = jnp.sum(jnp.where(met, 1.0, 0.0), axis=1, keepdims=True)
    share = jnp.maximum(counts, 1.0)
    row, col = iota((total, total // CAP), 0), iota((total, total // CAP), 1)
    col = (col % EV) * (MEM * CAP) + (col // EV) * CAP
    serve_of = [dot(serve, mask_bf(row == col + s))[0:1].astype(I32) for s in range(CAP)]

    landed(weights.at[pl.ds(0, (EV // 2 - 1) * block)], wr)
    own.wait()
    partner = e + 1 - 2 * lax.rem(e, 2)
    for hop in range(EV // 2):
        index = lax.rem(e + 2 * hop, EV)
        pltpu.make_async_remote_copy(
            part(index), part(index), ws, cr, device_id=(partner, m), device_id_type=MESH
        ).start()

    landed(rf, f2r)
    for chunk in fine:
        message = dot(route[chunk], rf[...].reshape(total, width)).astype(BF)
        xm[chunk] = message.reshape(EV, few * CAP, width)
        send_near(chunk, xm, nm, m1s, m1r)
    for chunk in fine:
        send_far(chunk, CAP, perm, nm, sm, rm, m2s, (m1r, m2r))
    finish_own(sm, rm, m2r)

    landed(weights.at[pl.ds(0, EV // 2 * block)], cr)
    landed(tails, e2r)
    arrived = tails[...].reshape(total // CAP, 128)
    encoded_sum, edge_sum = 0.0, []
    for s in range(CAP):
        hits = serve_of[s] == iota((nodes, total // CAP), 0)
        mine = column(serve_of[s]) == iota((total // CAP, nodes), 1)
        before = jnp.sum(jnp.where(mine, last_time[...].astype(F32), 0.0), axis=1, keepdims=True)
        digits = arrived[:, s * 64 : s * 64 + 64].astype(F32)
        time = digits[:, edges : edges + 1] * DIGIT + digits[:, edges + 1 : edges + 2]
        encoded = jnp.cos((time - before) * freq[...] + phase[...]).astype(BF)
        encoded_sum = encoded_sum + dot(mask_bf(hits), encoded)
        edge_sum.append(dot(mask_bf(hits), arrived))
    edge_sum = edge_sum[0] + pltpu.roll(edge_sum[1], 64, 1)
    encoded_mean = (encoded_sum / share).astype(BF)
    edge_mean = (edge_sum / share).astype(BF)
    w = 3 * width
    for t in range(3):
        third = pl.ds(t * width, width)
        pre_in[:, third] = (
            dot_t(memory[...], weights[third, 0:width])
            + dot_t(encoded_mean, weights[third, w : w + times])
            + dot_t(edge_mean, weights[third, w + 128 : w + 256])
            + bias[0:1, third]
        )
        pre_hid[:, third] = dot_t(memory[...], weights[third, 2 * width : 3 * width]) + bias[1:2, third]
    picks = spread(mask_bf(column(lookup_serve[...]) == iota((total_look, nodes), 1)), CAPN, WIDE)
    for c in range(WIDE):
        serve_look[c] = picks[:, c].reshape(total_look // WIDE, nodes)
    perm = reorder(CAPN, WIDE)

    landed(rm, m2r)
    summed = dot(matches[...], rm[...].reshape(total, width))
    averaged = (summed / share).astype(BF)

    def pre(t):
        third = pl.ds(t * width, width)
        return pre_in[:, third] + dot_t(averaged, weights[third, width : 2 * width])

    reset = jax.nn.sigmoid(pre(0) + pre_hid[:, 0:width])
    update = jax.nn.sigmoid(pre(1) + pre_hid[:, width : 2 * width])
    candidate = jnp.tanh(pre(2) + reset * pre_hid[:, 2 * width : 3 * width])
    previous = memory[...].astype(F32)
    fresh = (1.0 - update) * candidate + update * previous
    new_memory[...] = jnp.where(counts > 0, fresh, previous).astype(BF)

    for chunk in order:
        rows = dot(serve_look[chunk], new_memory[...]).astype(BF)
        xl[chunk] = rows.reshape(EV, MEM // WIDE * CAPN, width)
        send_near(chunk, xl, nl, l1s, l1r)
    result = pltpu.make_async_copy(new_memory, new_memory_out, store)
    result.start()
    hub = dot(mask_bf(hub_node[0] == iota((16, nodes), 1)), new_memory[...])
    hub_one[...] = jnp.concatenate(
        [hub[0:1, j * 128 : j * 128 + 128] for j in range(width // 128)], axis=0
    ).astype(BF)
    pltpu.make_async_copy(hub_one, hub_all.at[m], h1r).start()

    def hub_far(i, carry):
        t = mx * ZS + lax.rem(mz + i, ZS)
        pltpu.make_async_remote_copy(
            hub_one, hub_all.at[m], h1s, h1r, device_id=(e, t), device_id_type=MESH
        ).start()
        return carry

    lax.fori_loop(1, ZS, hub_far, 0)
    for chunk in order:
        send_far(chunk, CAPN, perm, nl, sl, looked, l2s, (l1r, l2r))
    finish_own(sl, looked, l2r)
    line = hub_all.at[pl.ds(mx * ZS, ZS)]
    landed(line, h1r)
    for dx in range(1, XS):
        pltpu.make_async_remote_copy(
            line, line, hxs, hxr, device_id=(e, lax.rem(mx + dx, XS) * ZS + mz), device_id_type=MESH
        ).start()
    landed(hub_all.at[pl.ds(0, (XS - 1) * ZS)], hxr)
    gathered = hub_all[...].astype(F32)
    hub_rows[...] = jnp.concatenate(
        [gathered[:, j, :] for j in range(width // 128)], axis=1
    ).astype(BF)
    pltpu.make_async_copy(hub_rows, hubs.at[e], h2r).start()

    def hub_near(i, carry):
        pltpu.make_async_remote_copy(
            hub_rows, hubs.at[e], h2s, h2r, device_id=(lax.rem(e + i, EV), m), device_id_type=MESH
        ).start()
        return carry

    lax.fori_loop(1, EV, hub_near, 0)

    routed = lookup_slot.shape[0]
    near = neighbour_gap.shape[0]
    for k in range(near):
        encoded = encode(column(neighbour_gap[k : k + 1]), freq[...], phase[...])
        keyenc[k] = dot(encoded, keyval_weight[width : width + times])
    still = jnp.broadcast_to(jnp.cos(phase[...]), (16, times)).astype(BF)
    query_enc[...] = dot(still, query_weight[width : width + times])
    for k in range(routed):
        at = column(arrival(lookup_slot[k : k + 1], CAPN))
        gather_look[pl.ds(k * events, events)] = mask_bf(at == iota((events, total_look), 1))
    landed(hubs, h2r)
    for k in range(near - routed + 1):
        choice = column(hub_choice[k : k + 1])
        rows = dot(mask_bf(choice == iota((events, DEVICES), 1)), hubs[...].reshape(DEVICES, width)).astype(BF)
        keyhub[k] = (dot(rows, keyval_weight[0:width]) + keyenc[routed - 1 + k]).astype(BF)

    landed(looked, l2r)
    everything = looked[...].reshape(total_look, width)
    own_row = dot(gather_look[0:events], everything).astype(BF)
    query = (dot(own_row, query_weight[0:width]) + query_enc[0:1]).astype(BF).astype(F32)
    att = query.shape[1]
    head = att // HEADS
    keyval = []
    for k in range(near):
        if k < routed - 1:
            rows = dot(gather_look[pl.ds((k + 1) * events, events)], everything).astype(BF)
            keyval.append((dot(rows, keyval_weight[0:width]) + keyenc[k]).astype(BF))
        else:
            keyval.append(keyhub[k - routed + 1])
    mixed = []
    for h in range(HEADS):
        q = query[:, h * head : h * head + head]
        scores = [
            jnp.sum(q * kv[:, h * head : h * head + head].astype(F32), axis=1, keepdims=True)
            * head ** (-0.5)
            for kv in keyval
        ]
        top = functools.reduce(jnp.maximum, scores)
        expo = [jnp.exp(x - top) for x in scores]
        base = functools.reduce(jnp.add, expo)
        acc = 0.0
        for x, kv in zip(expo, keyval):
            prob = (x / base).astype(BF).astype(F32)
            acc = acc + prob * kv[:, att + h * head : att + h * head + head].astype(F32)
        mixed.append(acc.astype(BF))
    mixed = jnp.concatenate(mixed, axis=1)
    embedding[...] = (
        dot(mixed, output_weight[0:att]) + dot(own_row, output_weight[att : att + width])
    ).astype(BF)

    drain(xf, rf, f1s, f2s)
    drain(xe, tails, e1s, e2s)
    drain(xm, rm, m1s, m2s)
    drain(xl, looked, l1s, l2s)
    landed(weights.at[pl.ds(0, (EV - 1) * block)], ws)
    landed(hub_all.at[pl.ds(0, ZS - 1)], h1s)
    landed(hub_all.at[pl.ds(0, (XS - 1) * ZS)], hxs)
    landed(hubs.at[pl.ds(0, EV - 1)], h2s)
    result.wait()


def vm(*shape, dtype=BF):
    return pltpu.VMEM(shape, dtype)


def path(slots, width, chunks):
    near = (chunks, EV, MEM // chunks * slots, width)
    far = (MEM, EV * slots, width)
    return [vm(*near), vm(*near), vm(*far), vm(*far)]


def sems(chunks):
    dma = pltpu.SemaphoreType.DMA
    return [dma, dma((chunks,)), dma, dma]


def local(
    memory,
    last_time,
    event_time,
    edge_features,
    update_slot,
    update_serve,
    lookup_slot,
    lookup_serve,
    neighbour_gap,
    hub_node,
    hub_choice,
    time_freq,
    time_phase,
    gru_weight,
    gru_bias,
    query_weight,
    keyval_weight,
    output_weight,
):
    nodes, width = memory.shape
    events = event_time.shape[0]
    gates = gru_bias.shape[1]
    padded = 3 * width + 256
    routed = lookup_slot.shape[1]
    near = neighbour_gap.shape[1]
    total, total_look = update_serve.shape[1], lookup_serve.shape[1]
    args = (
        update_serve, memory, event_time.reshape(1, -1), edge_features.T, update_slot.T, gru_weight.T,
        last_time.reshape(1, -1), lookup_slot.T, lookup_serve, neighbour_gap.T, hub_choice.T,
        time_freq.reshape(1, -1), time_phase.reshape(1, -1), gru_bias, query_weight, keyval_weight,
        output_weight,
    )
    dma = pltpu.SemaphoreType.DMA
    return tuple(pl.pallas_call(
        step_kernel,
        out_shape=[
            jax.ShapeDtypeStruct((nodes, width), BF),
            jax.ShapeDtypeStruct((events, width), BF),
        ],
        in_specs=[pl.BlockSpec(memory_space=pltpu.HBM)] * len(args)
        + [pl.BlockSpec(memory_space=pltpu.SMEM)],
        out_specs=[pl.BlockSpec(memory_space=pl.ANY), pl.BlockSpec(memory_space=pltpu.VMEM)],
        scratch_shapes=path(CAP, width, FINE) * 2 + path(1, 128, WIDE) + path(CAPN, width, WIDE)
        + [
            vm(gates // EV, padded),
            vm(gates, padded),
            vm(2 * events, total),
            vm(nodes, total),
            vm(nodes, gates, dtype=F32),
            vm(nodes, gates, dtype=F32),
            vm(width // 128, 128),
            vm(MEM, width // 128, 128),
            vm(MEM, width),
            vm(EV, MEM, width),
            vm(near, events, keyval_weight.shape[1], dtype=F32),
            vm(near - routed + 1, events, keyval_weight.shape[1]),
            vm(16, query_weight.shape[1], dtype=F32),
            vm(routed * events, total_look),
            vm(WIDE, total_look // WIDE, nodes),
            vm(FINE, total // FINE, total),
        ]
        + [vm(nodes, width)] + [vm(*a.shape, dtype=a.dtype) for a in args]
        + sems(FINE) + sems(WIDE) + sems(FINE) + sems(WIDE) + [dma] * 10 + [dma((len(args),)), dma],
        compiler_params=pltpu.CompilerParams(
            collective_id=0, has_side_effects=True, vmem_limit_bytes=62 << 20
        ),
    )(*args, hub_node))


def solution(mesh):
    both = ("ev", "mem")
    rows, flat = P(both, None), P(both)
    return jax.shard_map(
        local,
        mesh=mesh,
        in_specs=(
            rows, flat, flat, rows, rows, rows, rows, rows, rows, flat, rows,
            P(), P(), P(None, "ev"), P(), P(), P(), P(),
        ),
        out_specs=(rows, rows),
        check_vma=False,
    )
```

```python
import functools

import jax
import jax.numpy as jnp
from jax import lax
from jax.experimental import pallas as pl
from jax.experimental.pallas import tpu as pltpu
from jax.sharding import PartitionSpec as P

HEADS = 2
DIGIT = 32
EV, MEM, ZS, XS = 8, 64, 16, 4
WIDE, FINE = 8, 16
DEVICES = EV * MEM
CAP, CAPN = 2, 3
MESH = pl.DeviceIdType.MESH
BF = jnp.bfloat16
F32 = jnp.float32
I32 = jnp.int32


def dot(a, b):
    return jnp.dot(a, b, preferred_element_type=F32)


def dot_t(a, b):
    return lax.dot_general(a, b, (((1,), (1,)), ((), ())), preferred_element_type=F32)


def mask_bf(mask):
    return jnp.where(mask, 1.0, 0.0).astype(BF)


def iota(shape, dim):
    return lax.broadcasted_iota(I32, shape, dim)


def div(x, k):
    if k % 3 == 0:
        return ((x // (k // 3)) * 43691) >> 17
    return x // k


def place():
    e, m = lax.axis_index("ev"), lax.axis_index("mem")
    return e, m, m // ZS, lax.rem(m, ZS)


def greet():
    e, m, _, _ = place()
    barrier = pltpu.get_barrier_semaphore()

    def near(i, carry):
        pl.semaphore_signal(barrier, inc=1, device_id=(lax.rem(e + i, EV), m), device_id_type=MESH)
        return carry

    def far(i, carry):
        t = lax.rem(m + 1 + lax.rem(i + MEM // 2, MEM - 1), MEM)
        pl.semaphore_signal(barrier, inc=1, device_id=(e, t), device_id_type=MESH)
        return carry

    lax.fori_loop(0, MEM - 1, far, 0)
    lax.fori_loop(1, EV, near, 0)


def meet():
    pl.semaphore_wait(pltpu.get_barrier_semaphore(), EV + MEM - 2)


def landed(ref, sem):
    pltpu.make_async_copy(ref, ref, sem).wait()


def send_near(chunk, source, near, sent, came):
    e, m, _, _ = place()
    pltpu.make_async_copy(source.at[chunk, e], near.at[chunk, e], came.at[chunk]).start()

    def step(i, carry):
        t = lax.rem(e + i, EV)
        pltpu.make_async_remote_copy(
            source.at[chunk, t], near.at[chunk, e], sent, came.at[chunk],
            device_id=(t, m), device_id_type=MESH,
        ).start()
        return carry

    lax.fori_loop(1, EV, step, 0)


def reorder(slots, chunks):
    part = MEM // chunks
    n = EV * part * slots
    row, col = iota((n, n), 0), iota((n, n), 1)
    z, rest = div(row, EV * slots), row
    rest = row - z * (EV * slots)
    e = div(rest, slots)
    s = rest - e * slots
    return mask_bf(col == e * (part * slots) + z * slots + s)


def send_far(chunk, slots, perm, near, staged, result, sent, came):
    e, m, _, mz = place()
    part = MEM // near.shape[0]
    rows = EV * part * slots
    width = near.shape[-1]
    landed(near.at[chunk], came[0].at[chunk])
    block = dot(perm, near[chunk].reshape(rows, width)).astype(BF)
    staged[pl.ds(chunk * part, part)] = block.reshape(part, EV * slots, width)

    def step(i, carry):
        t = chunk * part + lax.rem(mz + i + part // 2, part)

        @pl.when(t != m)
        def _():
            pltpu.make_async_remote_copy(
                staged.at[t], result.at[m], sent, came[1], device_id=(e, t), device_id_type=MESH
            ).start()

        return carry

    lax.fori_loop(0, part, step, 0)


def finish_own(staged, result, came):
    _, m, _, _ = place()
    pltpu.make_async_copy(staged.at[m], result.at[m], came).start()


def drain(source, result, sent_near, sent_far):
    for c in range(source.shape[0]):
        landed(source.at[c, pl.ds(0, EV - 1)], sent_near)
    landed(result.at[pl.ds(0, MEM - 1)], sent_far)


def column(row):
    eye = iota((128, 128), 0) == iota((128, 128), 1)
    parts = []
    for b in range(row.shape[1] // 128):
        piece = row[:, b * 128 : b * 128 + 128].astype(F32)
        parts.append(jnp.sum(jnp.where(eye, piece, 0.0), axis=1, keepdims=True))
    return jnp.concatenate(parts, axis=0).astype(I32)


def arrival(slot, cap):
    device = div(slot, cap)
    at = slot - device * cap
    return (device % MEM) * (EV * cap) + (device // MEM) * cap + at


def spread(rows, slots, chunks):
    return rows.reshape(EV, chunks, MEM // chunks * slots, rows.shape[1])


def encode(gap, freq, phase):
    return jnp.cos(gap.astype(F32) * freq + phase).astype(BF)


def step_kernel(
    update_serve_in, memory_in, event_time_in, edge_in, update_slot_in, weight_in, last_time_in,
    lookup_slot_in, lookup_serve_in, neighbour_gap_in, hub_choice_in, freq_in, phase_in, bias_in,
    query_weight_in, keyval_weight_in, output_weight_in, hub_node,
    new_memory_out, embedding,
    xf, nf, sf, rf, xm, nm, sm, rm, xe, ne, se, tails, xl, nl, sl, looked,
    shard, weights, gather, matches, pre_in, pre_hid, hub_one, hub_all, hub_rows, hubs, keyenc, keyhub,
    query_enc, gather_look, serve_look, route, new_memory,
    update_serve, memory, event_time, edge, update_slot, weight, last_time, lookup_slot, lookup_serve,
    neighbour_gap, hub_choice, freq, phase, bias, query_weight, keyval_weight, output_weight,
    f1s, f1r, f2s, f2r, e1s, e1r, e2s, e2r, m1s, m1r, m2s, m2r, l1s, l1r, l2s, l2r,
    ws, wr, cs, cr, h1s, h1r, hxs, hxr, h2s, h2r, load, store,
):
    e, m, mx, mz = place()
    nodes, width = memory.shape
    events = event_time.shape[1]
    edges = edge.shape[0]
    times = freq.shape[1]
    total = MEM * EV * CAP
    total_look = MEM * EV * CAPN
    order = [
        lax.rem(mx + dx, XS) * 2 + lax.rem(mz // 8 + half, 2) for dx in (2, 1, 3, 0) for half in (1, 0)
    ]
    fine = [
        lax.rem(mx + dx, XS) * 4 + lax.rem(mz // 4 + dz, 4) for dx in (2, 1, 3, 0) for dz in (2, 1, 3, 0)
    ]

    greet()
    loads = [
        pltpu.make_async_copy(a, b, load.at[i])
        for i, (a, b) in enumerate([
            (update_serve_in, update_serve), (memory_in, memory), (event_time_in, event_time),
            (edge_in, edge), (update_slot_in, update_slot), (weight_in, weight), (last_time_in, last_time),
            (lookup_slot_in, lookup_slot), (lookup_serve_in, lookup_serve),
            (neighbour_gap_in, neighbour_gap), (hub_choice_in, hub_choice), (freq_in, freq),
            (phase_in, phase), (bias_in, bias), (query_weight_in, query_weight),
            (keyval_weight_in, keyval_weight), (output_weight_in, output_weight),
        ])
    ]
    for copy in loads:
        copy.start()
    loads[0].wait()
    pick = column(update_serve[...]) == iota((total, nodes), 1)
    loads[1].wait()
    rows = spread(dot(mask_bf(pick), memory[...]).astype(BF), CAP, FINE)
    for c in range(FINE):
        xf[c] = rows[:, c]
    meet()
    for chunk in fine:
        send_near(chunk, xf, nf, f1s, f1r)

    for copy in loads[2:5]:
        copy.wait()
    when = event_time[...]
    late = when // DIGIT
    packed = jnp.concatenate(
        [edge[...].astype(F32), late.astype(F32), (when - late * DIGIT).astype(F32),
         jnp.zeros((64 - edges - 2, events), F32)], axis=0
    )
    extra = jnp.concatenate([packed, packed], axis=0).T.astype(BF)
    slots = update_slot[...]
    target = iota((total // CAP, events), 0) * CAP
    tail = [
        dot(mask_bf((target + s == slots[0:1]) | (target + s == slots[1:2])), extra) for s in range(CAP)
    ]
    tail = jnp.where(iota(tail[0].shape, 1) < 64, tail[0], tail[1]).astype(BF)
    tail = spread(tail, 1, WIDE)
    for c in range(WIDE):
        xe[c] = tail[:, c]
    for chunk in order:
        send_near(chunk, xe, ne, e1s, e1r)

    for copy in loads[5:]:
        copy.wait()
    shard[:, 0 : 2 * width] = weight[:, 0 : 2 * width]
    rest = weight.shape[1] - 2 * width
    row, col = iota((rest, width + 256), 0), iota((rest, width + 256), 1)
    source = jnp.where(
        col < width, col + times + edges,
        jnp.where(col < width + 128, jnp.where(col < width + times, col - width, -1),
                  jnp.where(col < width + 128 + edges, col - width - 128 + times, -1)))
    shard[:, 2 * width :] = dot(weight[:, 2 * width :], mask_bf(row == source)).astype(BF)
    block = shard.shape[0]

    def part(index):
        return weights.at[pl.ds(pl.multiple_of(index * block, block), block)]

    own = pltpu.make_async_copy(shard, part(e), cs)
    own.start()
    for hop in range(1, EV // 2):
        pltpu.make_async_remote_copy(
            shard, part(e), ws, wr,
            device_id=(lax.rem(e + 2 * hop, EV), m), device_id_type=MESH,
        ).start()

    perm = reorder(CAP, FINE)
    perm_one = reorder(1, WIDE)
    for chunk in fine:
        send_far(chunk, CAP, perm, nf, sf, rf, f2s, (f1r, f2r))
    for chunk in order:
        send_far(chunk, 1, perm_one, ne, se, tails, e2s, (e1r, e2r))
    finish_own(sf, rf, f2r)
    finish_own(se, tails, e2r)

    places = arrival(slots, CAP)
    places = column(jnp.concatenate([places[1:2], places[0:1]], axis=1))
    gather[...] = mask_bf(places == iota((2 * events, total), 1))
    slot_row = jnp.concatenate([slots[0:1], slots[1:2]], axis=1)
    few = MEM // FINE
    for c in range(FINE):
        target = iota((EV * few * CAP, 1), 0)
        target = (target // (few * CAP)) * (MEM * CAP) + c * (few * CAP) + target % (few * CAP)
        route[c] = dot(mask_bf(target == slot_row), gather[...]).astype(BF)
    serve = jnp.broadcast_to(update_serve[...].astype(F32), (16, total)).astype(BF)
    row, col = iota((total, total), 0), iota((total, total), 1)
    col = ((col // CAP) % EV) * (MEM * CAP) + (col // (CAP * EV)) * CAP + col % CAP
    serve_in = dot(serve, mask_bf(row == col))[0:1].astype(I32)
    met = serve_in == iota((nodes, total), 0)
    matches[...] = mask_bf(met)
    counts = jnp.sum(jnp.where(met, 1.0, 0.0), axis=1, keepdims=True)
    share = jnp.maximum(counts, 1.0)
    row, col = iota((total, total // CAP), 0), iota((total, total // CAP), 1)
    col = (col % EV) * (MEM * CAP) + (col // EV) * CAP
    serve_of = [dot(serve, mask_bf(row == col + s))[0:1].astype(I32) for s in range(CAP)]

    landed(weights.at[pl.ds(0, (EV // 2 - 1) * block)], wr)
    own.wait()
    partner = e + 1 - 2 * lax.rem(e, 2)
    for hop in range(EV // 2):
        index = lax.rem(e + 2 * hop, EV)
        pltpu.make_async_remote_copy(
            part(index), part(index), ws, cr, device_id=(partner, m), device_id_type=MESH
        ).start()

    landed(rf, f2r)
    for chunk in fine:
        message = dot(route[chunk], rf[...].reshape(total, width)).astype(BF)
        xm[chunk] = message.reshape(EV, few * CAP, width)
        send_near(chunk, xm, nm, m1s, m1r)
    for chunk in fine:
        send_far(chunk, CAP, perm, nm, sm, rm, m2s, (m1r, m2r))
    finish_own(sm, rm, m2r)

    landed(weights.at[pl.ds(0, EV // 2 * block)], cr)
    landed(tails, e2r)
    arrived = tails[...].reshape(total // CAP, 128)
    encoded_sum, edge_sum = 0.0, []
    for s in range(CAP):
        hits = serve_of[s] == iota((nodes, total // CAP), 0)
        mine = column(serve_of[s]) == iota((total // CAP, nodes), 1)
        before = jnp.sum(jnp.where(mine, last_time[...].astype(F32), 0.0), axis=1, keepdims=True)
        digits = arrived[:, s * 64 : s * 64 + 64].astype(F32)
        time = digits[:, edges : edges + 1] * DIGIT + digits[:, edges + 1 : edges + 2]
        encoded = jnp.cos((time - before) * freq[...] + phase[...]).astype(BF)
        encoded_sum = encoded_sum + dot(mask_bf(hits), encoded)
        edge_sum.append(dot(mask_bf(hits), arrived))
    edge_sum = edge_sum[0] + pltpu.roll(edge_sum[1], 64, 1)
    encoded_mean = (encoded_sum / share).astype(BF)
    edge_mean = (edge_sum / share).astype(BF)
    w = 3 * width
    for t in range(3):
        third = pl.ds(t * width, width)
        pre_in[:, third] = (
            dot_t(memory[...], weights[third, 0:width])
            + dot_t(encoded_mean, weights[third, w : w + times])
            + dot_t(edge_mean, weights[third, w + 128 : w + 256])
            + bias[0:1, third]
        )
        pre_hid[:, third] = dot_t(memory[...], weights[third, 2 * width : 3 * width]) + bias[1:2, third]
    picks = spread(mask_bf(column(lookup_serve[...]) == iota((total_look, nodes), 1)), CAPN, WIDE)
    for c in range(WIDE):
        serve_look[c] = picks[:, c].reshape(total_look // WIDE, nodes)
    perm = reorder(CAPN, WIDE)

    landed(rm, m2r)
    summed = dot(matches[...], rm[...].reshape(total, width))
    averaged = (summed / share).astype(BF)

    def pre(t):
        third = pl.ds(t * width, width)
        return pre_in[:, third] + dot_t(averaged, weights[third, width : 2 * width])

    reset = jax.nn.sigmoid(pre(0) + pre_hid[:, 0:width])
    update = jax.nn.sigmoid(pre(1) + pre_hid[:, width : 2 * width])
    candidate = jnp.tanh(pre(2) + reset * pre_hid[:, 2 * width : 3 * width])
    previous = memory[...].astype(F32)
    fresh = (1.0 - update) * candidate + update * previous
    new_memory[...] = jnp.where(counts > 0, fresh, previous).astype(BF)

    for chunk in order:
        rows = dot(serve_look[chunk], new_memory[...]).astype(BF)
        xl[chunk] = rows.reshape(EV, MEM // WIDE * CAPN, width)
        send_near(chunk, xl, nl, l1s, l1r)
    result = pltpu.make_async_copy(new_memory, new_memory_out, store)
    result.start()
    hub = dot(mask_bf(hub_node[0] == iota((16, nodes), 1)), new_memory[...])
    hub_one[...] = jnp.concatenate(
        [hub[0:1, j * 128 : j * 128 + 128] for j in range(width // 128)], axis=0
    ).astype(BF)
    pltpu.make_async_copy(hub_one, hub_all.at[m], h1r).start()

    def hub_far(i, carry):
        t = mx * ZS + lax.rem(mz + i, ZS)
        pltpu.make_async_remote_copy(
            hub_one, hub_all.at[m], h1s, h1r, device_id=(e, t), device_id_type=MESH
        ).start()
        return carry

    lax.fori_loop(1, ZS, hub_far, 0)
    for chunk in order:
        send_far(chunk, CAPN, perm, nl, sl, looked, l2s, (l1r, l2r))
    finish_own(sl, looked, l2r)
    line = hub_all.at[pl.ds(mx * ZS, ZS)]
    landed(line, h1r)
    for dx in range(1, XS):
        pltpu.make_async_remote_copy(
            line, line, hxs, hxr, device_id=(e, lax.rem(mx + dx, XS) * ZS + mz), device_id_type=MESH
        ).start()
    landed(hub_all.at[pl.ds(0, (XS - 1) * ZS)], hxr)
    gathered = hub_all[...].astype(F32)
    hub_rows[...] = jnp.concatenate(
        [gathered[:, j, :] for j in range(width // 128)], axis=1
    ).astype(BF)
    pltpu.make_async_copy(hub_rows, hubs.at[e], h2r).start()

    def hub_near(i, carry):
        pltpu.make_async_remote_copy(
            hub_rows, hubs.at[e], h2s, h2r, device_id=(lax.rem(e + i, EV), m), device_id_type=MESH
        ).start()
        return carry

    lax.fori_loop(1, EV, hub_near, 0)

    routed = lookup_slot.shape[0]
    near = neighbour_gap.shape[0]
    for k in range(near):
        encoded = encode(column(neighbour_gap[k : k + 1]), freq[...], phase[...])
        keyenc[k] = dot(encoded, keyval_weight[width : width + times])
    still = jnp.broadcast_to(jnp.cos(phase[...]), (16, times)).astype(BF)
    query_enc[...] = dot(still, query_weight[width : width + times])
    for k in range(routed):
        at = column(arrival(lookup_slot[k : k + 1], CAPN))
        gather_look[pl.ds(k * events, events)] = mask_bf(at == iota((events, total_look), 1))
    landed(hubs, h2r)
    for k in range(near - routed + 1):
        choice = column(hub_choice[k : k + 1])
        rows = dot(mask_bf(choice == iota((events, DEVICES), 1)), hubs[...].reshape(DEVICES, width)).astype(BF)
        keyhub[k] = (dot(rows, keyval_weight[0:width]) + keyenc[routed - 1 + k]).astype(BF)

    landed(looked, l2r)
    everything = looked[...].reshape(total_look, width)
    own_row = dot(gather_look[0:events], everything).astype(BF)
    query = (dot(own_row, query_weight[0:width]) + query_enc[0:1]).astype(BF).astype(F32)
    att = query.shape[1]
    head = att // HEADS
    keyval = []
    for k in range(near):
        if k < routed - 1:
            rows = dot(gather_look[pl.ds((k + 1) * events, events)], everything).astype(BF)
            keyval.append((dot(rows, keyval_weight[0:width]) + keyenc[k]).astype(BF))
        else:
            keyval.append(keyhub[k - routed + 1])
    mixed = []
    for h in range(HEADS):
        q = query[:, h * head : h * head + head]
        scores = [
            jnp.sum(q * kv[:, h * head : h * head + head].astype(F32), axis=1, keepdims=True)
            * head ** (-0.5)
            for kv in keyval
        ]
        top = functools.reduce(jnp.maximum, scores)
        expo = [jnp.exp(x - top) for x in scores]
        base = functools.reduce(jnp.add, expo)
        acc = 0.0
        for x, kv in zip(expo, keyval):
            prob = (x / base).astype(BF).astype(F32)
            acc = acc + prob * kv[:, att + h * head : att + h * head + head].astype(F32)
        mixed.append(acc.astype(BF))
    mixed = jnp.concatenate(mixed, axis=1)
    embedding[...] = (
        dot(mixed, output_weight[0:att]) + dot(own_row, output_weight[att : att + width])
    ).astype(BF)

    drain(xf, rf, f1s, f2s)
    drain(xe, tails, e1s, e2s)
    drain(xm, rm, m1s, m2s)
    drain(xl, looked, l1s, l2s)
    landed(weights.at[pl.ds(0, (EV - 1) * block)], ws)
    landed(hub_all.at[pl.ds(0, ZS - 1)], h1s)
    landed(hub_all.at[pl.ds(0, (XS - 1) * ZS)], hxs)
    landed(hubs.at[pl.ds(0, EV - 1)], h2s)
    result.wait()


def vm(*shape, dtype=BF):
    return pltpu.VMEM(shape, dtype)


def path(slots, width, chunks):
    near = (chunks, EV, MEM // chunks * slots, width)
    far = (MEM, EV * slots, width)
    return [vm(*near), vm(*near), vm(*far), vm(*far)]


def sems(chunks):
    dma = pltpu.SemaphoreType.DMA
    return [dma, dma((chunks,)), dma, dma]


def local(
    memory,
    last_time,
    event_time,
    edge_features,
    update_slot,
    update_serve,
    lookup_slot,
    lookup_serve,
    neighbour_gap,
    hub_node,
    hub_choice,
    time_freq,
    time_phase,
    gru_weight,
    gru_bias,
    query_weight,
    keyval_weight,
    output_weight,
):
    nodes, width = memory.shape
    events = event_time.shape[0]
    gates = gru_bias.shape[1]
    padded = 3 * width + 256
    routed = lookup_slot.shape[1]
    near = neighbour_gap.shape[1]
    total, total_look = update_serve.shape[1], lookup_serve.shape[1]
    args = (
        update_serve, memory, event_time.reshape(1, -1), edge_features.T, update_slot.T, gru_weight.T,
        last_time.reshape(1, -1), lookup_slot.T, lookup_serve, neighbour_gap.T, hub_choice.T,
        time_freq.reshape(1, -1), time_phase.reshape(1, -1), gru_bias, query_weight, keyval_weight,
        output_weight,
    )
    dma = pltpu.SemaphoreType.DMA
    return tuple(pl.pallas_call(
        step_kernel,
        out_shape=[
            jax.ShapeDtypeStruct((nodes, width), BF),
            jax.ShapeDtypeStruct((events, width), BF),
        ],
        in_specs=[pl.BlockSpec(memory_space=pltpu.HBM)] * len(args)
        + [pl.BlockSpec(memory_space=pltpu.SMEM)],
        out_specs=[pl.BlockSpec(memory_space=pl.ANY), pl.BlockSpec(memory_space=pltpu.VMEM)],
        scratch_shapes=path(CAP, width, FINE) * 2 + path(1, 128, WIDE) + path(CAPN, width, WIDE)
        + [
            vm(gates // EV, padded),
            vm(gates, padded),
            vm(2 * events, total),
            vm(nodes, total),
            vm(nodes, gates, dtype=F32),
            vm(nodes, gates, dtype=F32),
            vm(width // 128, 128),
            vm(MEM, width // 128, 128),
            vm(MEM, width),
            vm(EV, MEM, width),
            vm(near, events, keyval_weight.shape[1], dtype=F32),
            vm(near - routed + 1, events, keyval_weight.shape[1]),
            vm(16, query_weight.shape[1], dtype=F32),
            vm(routed * events, total_look),
            vm(WIDE, total_look // WIDE, nodes),
            vm(FINE, total // FINE, total),
        ]
        + [vm(nodes, width)] + [vm(*a.shape, dtype=a.dtype) for a in args]
        + sems(FINE) + sems(WIDE) + sems(FINE) + sems(WIDE) + [dma] * 10 + [dma((len(args),)), dma],
        compiler_params=pltpu.CompilerParams(
            collective_id=0, has_side_effects=True, vmem_limit_bytes=62 << 20
        ),
    )(*args, hub_node))


def solution(mesh):
    both = ("ev", "mem")
    rows, flat = P(both, None), P(both)
    return jax.shard_map(
        local,
        mesh=mesh,
        in_specs=(
            rows, flat, flat, rows, rows, rows, rows, rows, rows, flat, rows,
            P(), P(), P(None, "ev"), P(), P(), P(), P(),
        ),
        out_specs=(rows, rows),
        check_vma=False,
    )
```
